128 devices in a mesh: dp: 8 (over z, y_lo), expert: 16 (over y_hi, x, core).
Axes of the slice: x: 4, y: 4 (y_hi: 2, y_lo: 2; y = y_hi * 2 + y_lo), z: 4, core: 2. Of those that a mesh axis runs over, the one named last changes fastest.
Arguments:
- tokens: bfloat16 [16384, 2048], P(('dp', 'expert')), may hold values from -120 to 120
- norm_gain: float32 [2048], replicated, may hold values from 0.1 to 1.9
- expert_ids: int32 [16384, 6], P(('dp', 'expert')), may hold values from 0 to 63, all different within a row; in each aligned block of 128 rows (0 to 127, 128 to 255, ...) at most 14 rows name the same one
- gate_weights: float32 [16384, 6], P(('dp', 'expert')), may hold values from 0.05 to 1
- gate_proj: bfloat16 [128, 2048, 704], P(('dp', 'expert')), may hold values from -0.125 to 0.125
- up_proj: bfloat16 [128, 2048, 704], P(('dp', 'expert')), may hold values from -0.125 to 0.125
- down_proj: bfloat16 [128, 704, 2048], P(('dp', 'expert')), may hold values from -0.15625 to 0.15625
- student_one: bfloat16 [2048, 4096], P(None, 'expert'), may hold values from -0.125 to 0.125
- student_two: bfloat16 [2048, 8192], P(None, 'expert'), may hold values from -0.125 to 0.125
- cot_one: bfloat16 [16384, 4096], P('dp', 'expert'), may hold values from -6 to 6
- cot_two: bfloat16 [16384, 8192], P('dp', 'expert'), may hold values from -6 to 6
Outputs:
- layer_out: bfloat16 [16384, 2048], P(('dp', 'expert'))
- feat_one: bfloat16 [16384, 4096], P('dp', 'expert')
- feat_two: bfloat16 [16384, 8192], P('dp', 'expert')
- grad_one: float32 [2048, 4096], P('dp', 'expert')
- grad_two: float32 [2048, 8192], P('dp', 'expert')
The draws below stay inside these ranges and needn't reach their ends.
Inputs may be any that keep to these rules, and one draw needn't show every extreme that they name: `expert_ids`: in each aligned block of 128 rows (the rows of one device) no expert is named by more than 14 entries; in every draw some expert is named by exactly 14 entries of some block.
All inputs are finite; a program needn't handle non-finite values.
Results may differ from the reference program's by a relative error of at most 0.0082.
Values may be sent and summed in bfloat16 or wider, within the bound.
No kernel may reach another device: no remote copies, remote signals or barrier semaphores. Data moves between devices by JAX's collectives and lax.ppermute only.
A program may use at most 128 MiB of HBM per device.

```python
import math
import jax
import jax.numpy as jnp
import numpy as np
from jax import lax

D = 2048
FE = 1408
TOP = 6
S1 = 4096
S2 = 8192
TOK_DEV = 128
EXPERTS = 64
CAP = 14
TOKENS = 16384


def draw_tokens(key, part):
    key_base, key_cols, key_rows = jax.random.split(key, 3)
    base = jnp.clip(jax.random.normal(key_base, (TOKENS, D), jnp.float32), -4.0, 4.0)
    rows_scale = jnp.exp(jax.random.uniform(key_rows, (TOKENS, 1), jnp.float32, math.log(0.3), math.log(3.0)))
    cols_scale = jnp.exp(jax.random.uniform(key_cols, (1, D), jnp.float32, 0.0, math.log(10.0)))
    return (base * cols_scale * rows_scale).astype(jnp.bfloat16)


def shard_levels(rng, dims, pieces, low, high):
    def one(position, shards_of):
        draws = jax.random.uniform(jax.random.fold_in(jax.random.fold_in(rng, 6), position), (shards_of,), jnp.float32, low / len(pieces), high / len(pieces))
        return jnp.repeat(jnp.exp(draws), dims[position] // shards_of).reshape((-1,) + (1,) * (len(dims) - position - 1))

    level = one(*pieces[0])
    for cut in pieces[1:]:
        level = level * one(*cut)
    return level


def shared_out(own_key, own, number, rows, count, top, most, skew):
    order = jax.random.permutation(own_key, count)
    crowded, common = portions_of(count, rows * top, most, skew, True), portions_of(count, rows * top, most, skew, False)
    places = jnp.arange(count)

    def named(tallies, rotation):
        used = int((tallies > 0).sum())
        fixed = max(1, used // 4)
        passed = fixed + (places - fixed + rotation * (used - fixed)) % max(1, count - fixed)
        return jnp.zeros((count,), jnp.int32).at[order[jnp.where(places < fixed, places, passed)]].set(jnp.asarray(tallies, jnp.int32))

    tallies = jnp.where(number % 4 == 0, named(crowded, number // 4), named(common, number - number // 4 - 1))
    mixed = jax.random.permutation(jax.random.fold_in(own, 3), count)
    source_of, receiver = mixed[0:count // 2 * 2:2], mixed[1:count // 2 * 2:2]
    slack = jnp.minimum(tallies[source_of] - 1, most - tallies[receiver]) // 2
    slack = jnp.where((source_of == order[0]) | (receiver == order[0]) | (tallies[receiver] == 0), 0, jnp.maximum(slack, 0))
    passed = jax.random.randint(jax.random.fold_in(own, 4), (count // 2,), 0, 1 << 20) % (slack + 1)
    tallies = tallies.at[source_of].add(-passed).at[receiver].add(passed)
    items = jnp.searchsorted(jnp.cumsum(tallies), jnp.arange(rows * top), side="right").astype(jnp.int32)
    listing = items.reshape(top, rows).T
    listing = listing[jax.random.permutation(jax.random.fold_in(own, 1), rows)]
    rotation = jax.random.randint(jax.random.fold_in(own, 2), (rows, 1), 0, top)
    return jnp.take_along_axis(listing, (jnp.arange(top)[None, :] + rotation) % top, axis=1)


def portions_of(count, total, most, skew, full):
    loads = [(1 << 20) // math.isqrt(standing ** skew) + 1 for standing in range(1, count + 1)]
    largest = most if full else min(most, max(-(-total // count), total * loads[0] // sum(loads)))
    least = 1 if total - largest >= count - 1 else 0
    given, spare = [largest] + [least] * (count - 1), total - largest - least * (count - 1)
    while spare > 0:
        free = [i for i in range(1, count) if given[i] < largest] or [i for i in range(1, count) if given[i] < most]
        pool, remaining = sum([loads[i] for i in free]), spare
        for i in free:
            extra = min(most - given[i], max(1, remaining * loads[i] // pool), spare)
            given[i] = given[i] + extra
            spare = spare - extra
    return np.array(given)


def gaussian(stream_key, dims, width, bound, cuts=(), kind=jnp.bfloat16):
    loudness = shard_levels(stream_key, dims, cuts, -0.22, 0.18) if cuts else 1.0
    array = jax.random.normal(stream_key, dims, jnp.float32) * width * loudness
    return jnp.minimum(jnp.maximum(array, -bound), bound).astype(kind)


def setup_inputs(seed: int = 0) -> dict:
    keys = jax.random.split(jax.random.key(seed), 12)
    tokens = draw_tokens(jax.random.fold_in(keys[11], 71), 0)
    norm_gain = jnp.clip(1.0 + 0.18 * jax.random.normal(keys[1], (D,), jnp.float32), 0.1, 1.9)
    expert_ids_keys = jax.random.split(jax.random.fold_in(keys[2], 1), TOKENS // TOK_DEV)
    expert_ids_turns = jax.random.permutation(jax.random.fold_in(keys[2], 3), TOKENS // TOK_DEV)
    expert_ids = jax.vmap(lambda own, number: shared_out(jax.random.fold_in(keys[2], 2), own, number, TOK_DEV, EXPERTS, TOP, CAP, 1))(expert_ids_keys, expert_ids_turns).reshape((TOKENS, TOP))
    gate_weights = jnp.clip(jnp.exp(math.log(1.0) - 2.9957323 * jax.random.uniform(keys[3], (TOKENS, TOP), jnp.float32) ** shard_levels(keys[3], (TOKENS, TOP), ((0, 128),), -0.2, 0.2)), 0.05, 1.0)
    gate_proj = gaussian(keys[4], (2 * EXPERTS, D, FE // 2), D ** -0.5, 0.125, ((0, 128),))
    up_proj = gaussian(keys[5], (2 * EXPERTS, D, FE // 2), D ** -0.5, 0.125, ((0, 128),))
    down_proj = gaussian(keys[6], (2 * EXPERTS, FE // 2, D), FE ** -0.5, 0.15625, ((0, 128),))
    student_one = gaussian(keys[7], (D, S1), D ** -0.5, 0.125, ((1, 16),))
    student_two = gaussian(keys[8], (D, S2), D ** -0.5, 0.125, ((1, 16),))
    cot_one = gaussian(keys[9], (TOKENS, S1), 1.0, 6.0, ((0, 8), (1, 16)))
    cot_two = gaussian(keys[10], (TOKENS, S2), 1.0, 6.0, ((0, 8), (1, 16)))
    return dict(tokens=tokens, norm_gain=norm_gain, expert_ids=expert_ids, gate_weights=gate_weights, gate_proj=gate_proj, up_proj=up_proj, down_proj=down_proj, student_one=student_one, student_two=student_two, cot_one=cot_one, cot_two=cot_two)


def reference(tokens, norm_gain, expert_ids, gate_weights, gate_proj, up_proj, down_proj, student_one, student_two, cot_one, cot_two):
    widened = tokens.astype(jnp.float32)
    mean_sq = lax.optimization_barrier(jnp.mean(widened * widened, axis=-1, keepdims=True))
    normed = (widened * lax.rsqrt(mean_sq + 1e-06) * norm_gain).astype(jnp.bfloat16)
    blocks = TOKENS // TOK_DEV
    flat_ids = expert_ids.reshape(blocks, TOK_DEV * TOP).astype(jnp.int32)
    one_hot = (flat_ids[:, :, None] == jnp.arange(EXPERTS, dtype=jnp.int32)[None, None, :]).astype(jnp.int32)
    earlier = jnp.cumsum(one_hot, axis=1).astype(jnp.int32) - one_hot
    slots = lax.optimization_barrier(jnp.sum(earlier * one_hot, axis=-1)).astype(jnp.int32)
    block_ids = jnp.arange(blocks, dtype=jnp.int32)[:, None]
    positions = ((flat_ids * blocks + block_ids) * CAP + slots).reshape(-1).astype(jnp.int32)
    token_ids = (jnp.arange(TOKENS * TOP, dtype=jnp.int32) // TOP).astype(jnp.int32)
    table_size = EXPERTS * blocks * CAP
    tok_of = jnp.zeros((table_size,), jnp.int32).at[positions].set(token_ids).reshape(EXPERTS, blocks * CAP)
    gate_of = jnp.zeros((table_size,), jnp.float32).at[positions].set(gate_weights.reshape(-1)).reshape(EXPERTS, blocks * CAP)
    occupied = jnp.zeros((table_size,), jnp.float32).at[positions].set(1.0).reshape(EXPERTS, blocks * CAP)

    def expert_step(carry, expert):
        index_row = tok_of[expert]
        gathered = normed[index_row] * occupied[expert][:, None].astype(jnp.bfloat16)
        total = jnp.zeros((blocks * CAP, D), jnp.float32)
        for half in range(2):
            half_idx = 2 * expert + half
            gate_val = jnp.dot(gathered, gate_proj[half_idx], preferred_element_type=jnp.float32)
            up_val = jnp.dot(gathered, up_proj[half_idx], preferred_element_type=jnp.float32)
            hidden = (jax.nn.silu(gate_val) * up_val).astype(jnp.bfloat16)
            partial_out = jnp.dot(hidden, down_proj[half_idx], preferred_element_type=jnp.float32).astype(jnp.bfloat16)
            total = total + partial_out.astype(jnp.float32)
        expert_out = lax.optimization_barrier(total.astype(jnp.bfloat16)).astype(jnp.float32)
        carry = carry.at[index_row].add(expert_out * gate_of[expert][:, None])
        return (carry, None)
    mixed_sum, _ = lax.scan(expert_step, jnp.zeros((TOKENS, D), jnp.float32), jnp.arange(EXPERTS, dtype=jnp.int32))
    layer_out = mixed_sum.astype(jnp.bfloat16)
    feat_one = jnp.dot(layer_out, student_one, preferred_element_type=jnp.float32).astype(jnp.bfloat16)
    feat_two = jnp.dot(layer_out, student_two, preferred_element_type=jnp.float32).astype(jnp.bfloat16)
    grad_scale = 1.0 / math.sqrt(TOKENS)
    grad_one = jnp.dot(layer_out.T, cot_one, preferred_element_type=jnp.float32) * grad_scale
    grad_two = jnp.dot(layer_out.T, cot_two, preferred_element_type=jnp.float32) * grad_scale
    return (layer_out, feat_one, feat_two, grad_one, grad_two)
```

```python
import functools
import math

import jax
import jax.numpy as jnp
from jax import lax
from jax.experimental import pallas as pl
from jax.experimental.pallas import tpu as pltpu
from jax.sharding import PartitionSpec as P

LANES = 128


def dispatch_body(ids_ref, tok_ref, gain_ref, out_ref, pos_ref, rows_ref, pos_smem, sem, *, experts, cap):
    top, toks = ids_ref.shape
    width = tok_ref.shape[1]
    sub = width // LANES
    expert_iota = lax.broadcasted_iota(jnp.int32, (experts, toks), 0)
    named = [(ids_ref[k : k + 1, :] == expert_iota).astype(jnp.float32) for k in range(top)]
    total = named[0]
    for k in range(1, top):
        total = total + named[k]
    row = lax.broadcasted_iota(jnp.int32, (toks, toks), 0)
    col = lax.broadcasted_iota(jnp.int32, (toks, toks), 1)
    before = (row < col).astype(jnp.bfloat16)
    earlier = jnp.dot(total.astype(jnp.bfloat16), before, preferred_element_type=jnp.float32)
    for k in range(top):
        slot = jnp.sum(earlier * named[k], axis=0, keepdims=True)
        pos_ref[k : k + 1, :] = ids_ref[k : k + 1, :] * cap + slot.astype(jnp.int32)
    copy = pltpu.make_async_copy(pos_ref, pos_smem, sem)
    copy.start()
    out_ref[...] = jnp.zeros_like(out_ref)
    wide = tok_ref[...].astype(jnp.float32)
    mean_sq = jnp.mean(wide * wide, axis=-1, keepdims=True)
    normed = wide * lax.rsqrt(mean_sq + 1e-06) * gain_ref[...]
    for j in range(sub):
        rows_ref[pl.ds(j, toks, stride=sub), :] = normed[:, j * LANES : (j + 1) * LANES]
    copy.wait()

    def place(t, carry):
        one = rows_ref[pl.ds(pl.multiple_of(t * sub, sub), sub), :].astype(jnp.bfloat16)
        for k in range(top):
            out_ref[pos_smem[k, t]] = one
        return carry

    lax.fori_loop(0, toks, place, 0, unroll=4)


def dispatch(ids, tokens, gain, experts, cap):
    top, toks = ids.shape
    width = tokens.shape[1]
    sub = width // LANES
    return pl.pallas_call(
        functools.partial(dispatch_body, experts=experts, cap=cap),
        name="dispatch",
        out_shape=(
            jax.ShapeDtypeStruct((experts * cap, sub, LANES), jnp.bfloat16),
            jax.ShapeDtypeStruct((top, toks), jnp.int32),
        ),
        scratch_shapes=[
            pltpu.VMEM((toks * sub, LANES), jnp.float32),
            pltpu.SMEM((top, toks), jnp.int32),
            pltpu.SemaphoreType.DMA,
        ],
    )(ids, tokens, gain)


def combine_body(pos_ref, gates_ref, rows_ref, out_ref, acc_ref):
    top, toks = pos_ref.shape
    sub = rows_ref.shape[1]

    def gather(t, carry):
        acc = rows_ref[pos_ref[0, t]].astype(jnp.float32) * gates_ref[0, t]
        for k in range(1, top):
            acc = acc + rows_ref[pos_ref[k, t]].astype(jnp.float32) * gates_ref[k, t]
        acc_ref[pl.ds(pl.multiple_of(t * sub, sub), sub), :] = acc
        return carry

    lax.fori_loop(0, toks, gather, 0, unroll=4)
    for j in range(sub):
        out_ref[:, j * LANES : (j + 1) * LANES] = acc_ref[pl.ds(j, toks, stride=sub), :].astype(jnp.bfloat16)


def combine(pos, gates, rows):
    top, toks = pos.shape
    sub = rows.shape[1]
    return pl.pallas_call(
        combine_body,
        name="combine",
        grid_spec=pltpu.PrefetchScalarGridSpec(
            num_scalar_prefetch=2,
            grid=(1,),
            in_specs=[pl.BlockSpec(rows.shape, lambda i, p, g: (0, 0, 0), pipeline_mode=pl.Buffered(1))],
            out_specs=pl.BlockSpec((toks, sub * LANES), lambda i, p, g: (0, 0), pipeline_mode=pl.Buffered(1)),
            scratch_shapes=[pltpu.VMEM((toks * sub, LANES), jnp.float32)],
        ),
        out_shape=jax.ShapeDtypeStruct((toks, sub * LANES), jnp.bfloat16),
    )(pos, gates, rows)


def half_expert(rows, gate, up, down):
    gate_val = lax.dot_general(rows, gate, (((1,), (0,)), ((), ())), preferred_element_type=jnp.float32)
    up_val = lax.dot_general(rows, up, (((1,), (0,)), ((), ())), preferred_element_type=jnp.float32)
    hidden = (jax.nn.silu(gate_val) * up_val).astype(jnp.bfloat16)
    return jnp.dot(hidden, down, preferred_element_type=jnp.float32).astype(jnp.bfloat16)


def local(
    tokens,
    norm_gain,
    expert_ids,
    gate_weights,
    gate_proj,
    up_proj,
    down_proj,
    student_one,
    student_two,
    cot_one,
    cot_two,
):
    tok_dev, model_width = tokens.shape
    top_count = expert_ids.shape[1]
    devices = lax.axis_size("dp") * lax.axis_size("expert")
    experts = devices // 2
    capacity = 2 * ((tok_dev * top_count * 7 + 12 * experts - 1) // (12 * experts))
    sub = model_width // LANES
    partner = [(i, i ^ 1) for i in range(lax.axis_size("expert"))]
    other_gate = lax.ppermute(jnp.swapaxes(gate_proj[0], 0, 1), "expert", partner)
    other_up = lax.ppermute(jnp.swapaxes(up_proj[0], 0, 1), "expert", partner)
    other_down = lax.ppermute(down_proj[0], "expert", partner)

    placed, positions = dispatch(expert_ids.T, tokens, norm_gain.reshape(1, -1), experts, capacity)
    received = lax.all_to_all(
        placed.reshape(devices, capacity // 2, sub, LANES),
        ("dp", "expert"),
        split_axis=0,
        concat_axis=0,
        tiled=True,
    )
    flat_rows = received.reshape(devices * capacity // 2, model_width)
    first = half_expert(flat_rows, gate_proj[0], up_proj[0], down_proj[0])
    second = half_expert(flat_rows, other_gate.T, other_up.T, other_down)
    expert_out = (first.astype(jnp.float32) + second.astype(jnp.float32)).astype(jnp.bfloat16)
    returned = lax.all_to_all(
        expert_out.reshape(devices, capacity // 2, sub, LANES),
        ("dp", "expert"),
        split_axis=0,
        concat_axis=0,
        tiled=True,
    )
    layer_out = combine(positions, gate_weights.T, returned.reshape(experts * capacity, sub, LANES))
    gathered = lax.all_gather(layer_out, "expert", axis=0, tiled=True)
    feat_one = jnp.dot(gathered, student_one, preferred_element_type=jnp.float32).astype(jnp.bfloat16)
    feat_two = jnp.dot(gathered, student_two, preferred_element_type=jnp.float32).astype(jnp.bfloat16)
    cotangents = jnp.concatenate([cot_one, cot_two], axis=1)
    grad_scale = 1.0 / math.sqrt(gathered.shape[0] * lax.axis_size("dp"))
    terms = lax.dot_general(
        gathered, cotangents, (((0,), (0,)), ((), ())), preferred_element_type=jnp.float32
    )
    batches = lax.axis_size("dp")
    pieces = (terms * grad_scale).astype(jnp.bfloat16).reshape(batches, model_width // batches, -1)
    pieces = lax.all_to_all(pieces, "dp", split_axis=0, concat_axis=0, tiled=True)
    grads = jnp.sum(pieces.astype(jnp.float32), axis=0)
    split_at = student_one.shape[1]
    return (layer_out, feat_one, feat_two, grads[:, :split_at], grads[:, split_at:])


def solution(mesh):
    return jax.shard_map(
        local,
        mesh=mesh,
        in_specs=(
            P(("dp", "expert"), None),
            P(),
            P(("dp", "expert"), None),
            P(("dp", "expert"), None),
            P(("dp", "expert"), None, None),
            P(("dp", "expert"), None, None),
            P(("dp", "expert"), None, None),
            P(None, "expert"),
            P(None, "expert"),
            P("dp", "expert"),
            P("dp", "expert"),
        ),
        out_specs=(
            P(("dp", "expert"), None),
            P("dp", "expert"),
            P("dp", "expert"),
            P("dp", "expert"),
            P("dp", "expert"),
        ),
        check_vma=False,
    )
```

```python
import functools
import math

import jax
import jax.numpy as jnp
from jax import lax
from jax.experimental import pallas as pl
from jax.experimental.pallas import tpu as pltpu
from jax.sharding import PartitionSpec as P

LANES = 128


def dispatch_body(ids_ref, tok_ref, gain_ref, out_ref, pos_ref, rows_ref, pos_smem, sem, *, experts, cap):
    top, toks = ids_ref.shape
    width = tok_ref.shape[1]
    sub = width // LANES
    expert_iota = lax.broadcasted_iota(jnp.int32, (experts, toks), 0)
    named = [(ids_ref[k : k + 1, :] == expert_iota).astype(jnp.float32) for k in range(top)]
    total = named[0]
    for k in range(1, top):
        total = total + named[k]
    row = lax.broadcasted_iota(jnp.int32, (toks, toks), 0)
    col = lax.broadcasted_iota(jnp.int32, (toks, toks), 1)
    before = (row < col).astype(jnp.bfloat16)
    earlier = jnp.dot(total.astype(jnp.bfloat16), before, preferred_element_type=jnp.float32)
    for k in range(top):
        slot = jnp.sum(earlier * named[k], axis=0, keepdims=True)
        pos_ref[k : k + 1, :] = ids_ref[k : k + 1, :] * cap + slot.astype(jnp.int32)
    copy = pltpu.make_async_copy(pos_ref, pos_smem, sem)
    copy.start()
    out_ref[...] = jnp.zeros_like(out_ref)
    wide = tok_ref[...].astype(jnp.float32)
    mean_sq = jnp.mean(wide * wide, axis=-1, keepdims=True)
    normed = wide * lax.rsqrt(mean_sq + 1e-06) * gain_ref[...]
    for j in range(sub):
        rows_ref[pl.ds(j, toks, stride=sub), :] = normed[:, j * LANES : (j + 1) * LANES]
    copy.wait()

    def place(t, carry):
        one = rows_ref[pl.ds(pl.multiple_of(t * sub, sub), sub), :].astype(jnp.bfloat16)
        for k in range(top):
            out_ref[pos_smem[k, t]] = one
        return carry

    lax.fori_loop(0, toks, place, 0, unroll=4)


def dispatch(ids, tokens, gain, experts, cap):
    top, toks = ids.shape
    width = tokens.shape[1]
    sub = width // LANES
    return pl.pallas_call(
        functools.partial(dispatch_body, experts=experts, cap=cap),
        name="dispatch",
        out_shape=(
            jax.ShapeDtypeStruct((experts * cap, sub, LANES), jnp.bfloat16),
            jax.ShapeDtypeStruct((top, toks), jnp.int32),
        ),
        scratch_shapes=[
            pltpu.VMEM((toks * sub, LANES), jnp.float32),
            pltpu.SMEM((top, toks), jnp.int32),
            pltpu.SemaphoreType.DMA,
        ],
    )(ids, tokens, gain)


def combine_body(pos_ref, gates_ref, rows_ref, out_ref, acc_ref):
    top, toks = pos_ref.shape
    sub = rows_ref.shape[1]

    def gather(t, carry):
        acc = rows_ref[pos_ref[0, t]].astype(jnp.float32) * gates_ref[0, t]
        for k in range(1, top):
            acc = acc + rows_ref[pos_ref[k, t]].astype(jnp.float32) * gates_ref[k, t]
        acc_ref[pl.ds(pl.multiple_of(t * sub, sub), sub), :] = acc
        return carry

    lax.fori_loop(0, toks, gather, 0, unroll=4)
    for j in range(sub):
        out_ref[:, j * LANES : (j + 1) * LANES] = acc_ref[pl.ds(j, toks, stride=sub), :].astype(jnp.bfloat16)


def combine(pos, gates, rows):
    top, toks = pos.shape
    sub = rows.shape[1]
    return pl.pallas_call(
        combine_body,
        name="combine",
        grid_spec=pltpu.PrefetchScalarGridSpec(
            num_scalar_prefetch=2,
            grid=(1,),
            in_specs=[pl.BlockSpec(rows.shape, lambda i, p, g: (0, 0, 0), pipeline_mode=pl.Buffered(1))],
            out_specs=pl.BlockSpec((toks, sub * LANES), lambda i, p, g: (0, 0), pipeline_mode=pl.Buffered(1)),
            scratch_shapes=[pltpu.VMEM((toks * sub, LANES), jnp.float32)],
        ),
        out_shape=jax.ShapeDtypeStruct((toks, sub * LANES), jnp.bfloat16),
    )(pos, gates, rows)


def expert_body(rows_hbm, gate0, up0, down0, gate1, up1, down1, out_hbm,
                rows_ref, x_ref, acc_ref, gate_ref, up_ref, down_ref, hid_ref, in_sem, w_sem, out_sem, *, step, tile, cols):
    count, sub, _ = rows_hbm.shape
    hidden, width = down0.shape
    chunks = count // step
    ins = [
        pltpu.make_async_copy(rows_hbm.at[pl.ds(i * step, step)], rows_ref.at[pl.ds(i * step, step)], in_sem.at[i])
        for i in range(chunks)
    ]
    gates = [pltpu.make_async_copy(w, gate_ref.at[h], w_sem.at[h, 0]) for h, w in enumerate((gate0, gate1))]
    ups = [pltpu.make_async_copy(w, up_ref.at[h], w_sem.at[h, 1]) for h, w in enumerate((up0, up1))]
    downs = [pltpu.make_async_copy(w, down_ref.at[h], w_sem.at[h, 2]) for h, w in enumerate((down0, down1))]
    for c in ins[:2]:
        c.start()
    gates[0].start()
    for c in ins[2:]:
        c.start()
    for c in (ups[0], gates[1], ups[1], downs[0], downs[1]):
        c.start()
    for i in range(chunks):
        ins[i].wait()
        acc_ref[pl.ds(0, step * sub), :] = rows_ref[pl.ds(i * step, step)].astype(jnp.float32).reshape(step * sub, LANES)
        for j in range(sub):
            x_ref[pl.ds(i * step, step), j * LANES : (j + 1) * LANES] = acc_ref[
                pl.ds(j, step, stride=sub), :
            ].astype(jnp.bfloat16)
    contract = (((1,), (1,)), ((), ()))
    for h in range(2):
        gates[h].wait()
        ups[h].wait()
        for lo in range(0, hidden, tile):
            n = min(tile, hidden - lo)
            gate_val = lax.dot_general(x_ref[...], gate_ref[h, pl.ds(lo, n), :], contract, preferred_element_type=jnp.float32)
            up_val = lax.dot_general(x_ref[...], up_ref[h, pl.ds(lo, n), :], contract, preferred_element_type=jnp.float32)
            hid_ref[h, :, lo : lo + n] = (gate_val / (1.0 + jnp.exp(-gate_val)) * up_val).astype(jnp.bfloat16)
    for c in downs:
        c.wait()

    def down_step(d, carry):
        at = pl.ds(pl.multiple_of(d * cols, cols), cols)
        first = jnp.dot(hid_ref[0], down_ref[0, :, at], preferred_element_type=jnp.float32).astype(jnp.bfloat16)
        second = jnp.dot(hid_ref[1], down_ref[1, :, at], preferred_element_type=jnp.float32).astype(jnp.bfloat16)
        both = first.astype(jnp.float32) + second.astype(jnp.float32)
        for j in range(cols // LANES):
            acc_ref[pl.ds(d * (cols // LANES) + j, count, stride=sub), :] = both[:, j * LANES : (j + 1) * LANES]
        return carry

    lax.fori_loop(0, width // cols, down_step, 0)
    outs = [
        pltpu.make_async_copy(rows_ref.at[pl.ds(i * step, step)], out_hbm.at[pl.ds(i * step, step)], out_sem.at[i])
        for i in range(chunks)
    ]
    for i in range(chunks):
        rows_ref[pl.ds(i * step, step)] = (
            acc_ref[pl.ds(i * step * sub, step * sub), :].reshape(step, sub, LANES).astype(jnp.bfloat16)
        )
        outs[i].start()
    for c in outs:
        c.wait()


def expert(rows, gate0, up0, down0, gate1, up1, down1, step=128, tile=256, cols=256):
    count, sub, _ = rows.shape
    hidden, width = down0.shape
    chunks = count // step
    anywhere = pl.BlockSpec(memory_space=pl.ANY)
    return pl.pallas_call(
        functools.partial(expert_body, step=step, tile=tile, cols=cols),
        name="expert",
        in_specs=[anywhere] * 7,
        out_specs=anywhere,
        out_shape=jax.ShapeDtypeStruct(rows.shape, jnp.bfloat16),
        scratch_shapes=[
            pltpu.VMEM(rows.shape, jnp.bfloat16),
            pltpu.VMEM((count, width), jnp.bfloat16),
            pltpu.VMEM((count * sub, LANES), jnp.float32),
            pltpu.VMEM((2, hidden, width), jnp.bfloat16),
            pltpu.VMEM((2, hidden, width), jnp.bfloat16),
            pltpu.VMEM((2, hidden, width), jnp.bfloat16),
            pltpu.VMEM((2, count, hidden), jnp.bfloat16),
            pltpu.SemaphoreType.DMA((chunks,)),
            pltpu.SemaphoreType.DMA((2, 3)),
            pltpu.SemaphoreType.DMA((chunks,)),
        ],
        compiler_params=pltpu.CompilerParams(vmem_limit_bytes=60 * 1024 * 1024),
    )(rows, gate0, up0, down0, gate1, up1, down1)


def fetch_rows(at_ref, pieces, rows_ref, sem):
    copies = []
    for i, piece in enumerate(pieces):
        to = pl.ds(pl.multiple_of(at_ref[i], piece.shape[0]), piece.shape[0])
        copies.append(pltpu.make_async_copy(piece, rows_ref.at[to], sem.at[i]))
    return copies


def features_of(rows_ref, one_ref, two_ref, out_one, out_two):
    out_one[...] = jnp.dot(rows_ref[...], one_ref[...], preferred_element_type=jnp.float32).astype(jnp.bfloat16)
    width = two_ref.shape[1] // 2
    for j in range(2):
        at = slice(j * width, (j + 1) * width)
        out_two[:, at] = jnp.dot(
            rows_ref[...], two_ref[:, at], preferred_element_type=jnp.float32
        ).astype(jnp.bfloat16)


def near_body(at_ref, *refs, pieces):
    parts = refs[:pieces]
    one_hbm, two_hbm, cot_hbm, feat_one, feat_two, terms_hbm = refs[pieces : pieces + 6]
    rows_ref, one_ref, two_ref, cot_ref, acc_ref, out_one, out_two, sem, w_sem, out_sem = refs[pieces + 6 :]
    count = rows_ref.shape[0]
    start = pl.multiple_of(at_ref[pieces], count)
    loads = fetch_rows(at_ref, parts, rows_ref, sem)
    w_loads = [
        pltpu.make_async_copy(cot_hbm.at[:, pl.ds(start, count)], cot_ref, w_sem.at[0]),
        pltpu.make_async_copy(one_hbm, one_ref, w_sem.at[1]),
        pltpu.make_async_copy(two_hbm, two_ref, w_sem.at[2]),
    ]
    for c in loads + w_loads:
        c.start()
    for c in loads:
        c.wait()
    w_loads[0].wait()
    cols = 256
    tiles = acc_ref.shape[1] // cols
    outs = []
    for d in range(tiles):
        at = slice(d * cols, (d + 1) * cols)
        acc_ref[:, at] = jnp.dot(cot_ref[...], rows_ref[:, at], preferred_element_type=jnp.float32)
        outs.append(pltpu.make_async_copy(acc_ref.at[:, at], terms_hbm.at[:, at], out_sem.at[d]))
        outs[-1].start()
    w_loads[1].wait()
    w_loads[2].wait()
    features_of(rows_ref, one_ref, two_ref, out_one, out_two)
    outs.append(pltpu.make_async_copy(out_one, feat_one.at[pl.ds(start, count)], out_sem.at[tiles]))
    outs.append(pltpu.make_async_copy(out_two, feat_two.at[pl.ds(start, count)], out_sem.at[tiles + 1]))
    outs[-2].start()
    outs[-1].start()
    for c in outs:
        c.wait()


def far_terms_body(at_ref, *refs, pieces, scale):
    parts = refs[:pieces]
    cot_hbm, near_hbm, out_hbm, all_rows = refs[pieces : pieces + 4]
    rows_ref, cot_ref, acc_ref, cut_ref, sem, w_sem, acc_sem, out_sem = refs[pieces + 4 :]
    count = rows_ref.shape[0]
    start = pl.multiple_of(at_ref[pieces], count)
    loads = fetch_rows(at_ref, parts, rows_ref, sem)
    cot_load = pltpu.make_async_copy(cot_hbm.at[:, pl.ds(start, count)], cot_ref, w_sem.at[0])
    owners, _, cols = cut_ref.shape
    near = [
        pltpu.make_async_copy(near_hbm.at[:, d * cols : (d + 1) * cols], acc_ref.at[d], acc_sem.at[d])
        for d in range(owners)
    ]
    for c in loads:
        c.start()
    cot_load.start()
    for c in near:
        c.start()
    for c in loads:
        c.wait()
    keep = pltpu.make_async_copy(rows_ref, all_rows, w_sem.at[1])
    keep.start()
    cot_load.wait()
    outs = []
    for d in range(owners):
        far = jnp.dot(cot_ref[...], rows_ref[:, d * cols : (d + 1) * cols], preferred_element_type=jnp.float32)
        near[d].wait()
        cut_ref[d] = ((far + acc_ref[d]) * scale).astype(jnp.bfloat16)
        outs.append(pltpu.make_async_copy(cut_ref.at[d], out_hbm.at[d], out_sem.at[d]))
        outs[-1].start()
    for c in outs:
        c.wait()
    keep.wait()


def far_features_body(at_ref, rows_hbm, one_hbm, two_hbm, old_one, old_two, feat_one, feat_two, rows_ref, one_ref, two_ref, out_one, out_two, sem):
    count = rows_ref.shape[0]
    start = pl.multiple_of(at_ref[0], count)
    loads = [
        pltpu.make_async_copy(rows_hbm, rows_ref, sem.at[0]),
        pltpu.make_async_copy(one_hbm, one_ref, sem.at[1]),
        pltpu.make_async_copy(two_hbm, two_ref, sem.at[2]),
    ]
    for c in loads:
        c.start()
    for c in loads:
        c.wait()
    features_of(rows_ref, one_ref, two_ref, out_one, out_two)
    outs = [
        pltpu.make_async_copy(out_one, feat_one.at[pl.ds(start, count)], sem.at[3]),
        pltpu.make_async_copy(out_two, feat_two.at[pl.ds(start, count)], sem.at[4]),
    ]
    for c in outs:
        c.start()
    for c in outs:
        c.wait()


def sum_terms_body(pieces_ref, one_ref, two_ref):
    split = one_ref.shape[1]
    total = pieces_ref[0].astype(jnp.float32)
    for i in range(1, pieces_ref.shape[0]):
        total = total + pieces_ref[i].astype(jnp.float32)
    one_ref[...] = total[:split].T
    two_ref[...] = total[split:].T


VMEM_LIMIT = 60 * 1024 * 1024


def on_device(body, name, scalars, operands, out_shape, scratch, aliases=None, flops=0):
    anywhere = pl.BlockSpec(memory_space=pl.ANY)
    return pl.pallas_call(
        body,
        name=name,
        grid_spec=pltpu.PrefetchScalarGridSpec(
            num_scalar_prefetch=1,
            grid=(1,),
            in_specs=[anywhere] * len(operands),
            out_specs=tuple(anywhere for _ in out_shape),
            scratch_shapes=scratch,
        ),
        out_shape=out_shape,
        input_output_aliases=aliases or {},
        compiler_params=pltpu.CompilerParams(vmem_limit_bytes=VMEM_LIMIT),
        cost_estimate=pl.CostEstimate(flops=flops, transcendentals=0, bytes_accessed=12 << 20),
    )(scalars, *operands)


def project(layer_out, student_one, student_two, cots, move, place):
    rows, width = layer_out.shape
    y_hi, x, core = place
    half = rows // 2
    ring = 4
    group = 2 * ring * rows
    cols = student_one.shape[1] + student_two.shape[1]

    def around(own):
        right = move(own, 0, 1, 0)
        left = move(own, 0, -1, 0)
        far_right = move(right[:half], 0, 1, 0)
        far_left = move(left[half:], 0, -1, 0)
        return [own, right, left, far_right, far_left]

    def spots(base):
        at = [x, (x + ring - 1) % ring, (x + 1) % ring, (x + 2) % ring, (x + 2) % ring]
        at = [p * (2 * rows) for p in at]
        at[4] = at[4] + half
        return jnp.stack([p + c * rows for c in (core, 1 - core) for p in at] + [base]).astype(jnp.int32)

    up_way = move(layer_out[:half], 1, 0, 0)
    down_way = move(layer_out[half:], -1, 0, 0)
    near = around(layer_out)
    up_way = move(up_way, 1, 0, 0)
    down_way = move(down_way, -1, 0, 0)
    far = around(jnp.concatenate([up_way, down_way], axis=0))
    near = near + [move(p, 0, 0, 1) for p in near]
    far = far + [move(p, 0, 0, 1) for p in far]
    bf16, f32 = jnp.bfloat16, jnp.float32
    dma = pltpu.SemaphoreType.DMA
    total = 2 * group
    feat_shapes = (
        jax.ShapeDtypeStruct((total, student_one.shape[1]), bf16),
        jax.ShapeDtypeStruct((total, student_two.shape[1]), bf16),
    )
    w_vmem = [pltpu.VMEM(student_one.shape, bf16), pltpu.VMEM(student_two.shape, bf16)]
    out_vmem = [pltpu.VMEM((group, student_one.shape[1]), bf16), pltpu.VMEM((group, student_two.shape[1]), bf16)]
    work = 2 * group * width * cols
    feat_one, feat_two, terms = on_device(
        functools.partial(near_body, pieces=10),
        "near_rows",
        spots(y_hi * group),
        near + [student_one, student_two, cots],
        feat_shapes + (jax.ShapeDtypeStruct((cols, width), f32),),
        [pltpu.VMEM((group, width), bf16)]
        + w_vmem
        + [pltpu.VMEM((cols, group), bf16), pltpu.VMEM((cols, width), f32)]
        + out_vmem
        + [dma((10,)), dma((3,)), dma((width // 256 + 2,))],
        flops=2 * work,
    )
    owners = 8
    cut, far_rows = on_device(
        functools.partial(far_terms_body, pieces=10, scale=1.0 / math.sqrt(total * owners)),
        "far_terms",
        spots((1 - y_hi) * group),
        far + [cots, terms],
        (jax.ShapeDtypeStruct((owners, cols, width // owners), bf16), jax.ShapeDtypeStruct((group, width), bf16)),
        [
            pltpu.VMEM((group, width), bf16),
            pltpu.VMEM((cols, group), bf16),
            pltpu.VMEM((owners, cols, width // owners), f32),
            pltpu.VMEM((owners, cols, width // owners), bf16),
            dma((10,)),
            dma((2,)),
            dma((owners,)),
            dma((owners,)),
        ],
        flops=work,
    )
    pieces = lax.all_to_all(cut, "dp", split_axis=0, concat_axis=0, tiled=True)
    feat_one, feat_two = on_device(
        far_features_body,
        "far_features",
        ((1 - y_hi) * group).reshape(1).astype(jnp.int32),
        [far_rows, student_one, student_two, feat_one, feat_two],
        feat_shapes,
        [pltpu.VMEM((group, width), bf16)] + w_vmem + out_vmem + [dma((5,))],
        aliases={4: 0, 5: 1},
        flops=work,
    )
    split = student_one.shape[1]
    grad_one, grad_two = pl.pallas_call(
        sum_terms_body,
        name="sum_terms",
        out_shape=(
            jax.ShapeDtypeStruct((width // owners, split), f32),
            jax.ShapeDtypeStruct((width // owners, cols - split), f32),
        ),
    )(pieces)
    return feat_one, feat_two, grad_one, grad_two


def local(
    tokens,
    norm_gain,
    expert_ids,
    gate_weights,
    gate_proj,
    up_proj,
    down_proj,
    student_one,
    student_two,
    cot_one,
    cot_two,
):
    tok_dev, model_width = tokens.shape
    top_count = expert_ids.shape[1]
    devices = lax.axis_size("dp") * lax.axis_size("expert")
    experts = devices // 2
    capacity = 2 * ((tok_dev * top_count * 7 + 12 * experts - 1) // (12 * experts))
    sub = model_width // LANES
    axes = ("dp", "expert")
    index = lax.axis_index(axes)

    def move(array, y, x, core):
        def target(d):
            z, y_lo, y_hi, at_x, at_core = d // 32, d // 16 % 2, d // 8 % 2, d // 2 % 4, d % 2
            to_y = (y_hi * 2 + y_lo + y) % 4
            return z * 32 + to_y % 2 * 16 + to_y // 2 * 8 + (at_x + x) % 4 * 2 + (at_core + core) % 2

        return lax.ppermute(array, axes, [(d, target(d)) for d in range(devices)])

    cots = jnp.concatenate([cot_one, cot_two], axis=1).T
    other_gate = move(jnp.swapaxes(gate_proj[0], 0, 1), 0, 0, 1)
    other_up = move(jnp.swapaxes(up_proj[0], 0, 1), 0, 0, 1)
    other_down = move(down_proj[0], 0, 0, 1)

    placed, positions = dispatch(expert_ids.T, tokens, norm_gain.reshape(1, -1), experts, capacity)
    received = lax.all_to_all(
        placed.reshape(devices, capacity // 2, sub, LANES),
        ("dp", "expert"),
        split_axis=0,
        concat_axis=0,
        tiled=True,
    )
    expert_out = expert(
        received.reshape(devices * capacity // 2, sub, LANES),
        jnp.swapaxes(gate_proj[0], 0, 1),
        jnp.swapaxes(up_proj[0], 0, 1),
        down_proj[0],
        other_gate,
        other_up,
        other_down,
    )
    returned = lax.all_to_all(
        expert_out.reshape(devices, capacity // 2, sub, LANES),
        ("dp", "expert"),
        split_axis=0,
        concat_axis=0,
        tiled=True,
    )
    layer_out = combine(positions, gate_weights.T, returned.reshape(experts * capacity, sub, LANES))
    feat_one, feat_two, grad_one, grad_two = project(
        layer_out, student_one, student_two, cots, move, (index // 8 % 2, index // 2 % 4, index % 2)
    )
    return (layer_out, feat_one, feat_two, grad_one, grad_two)


def solution(mesh):
    return jax.shard_map(
        local,
        mesh=mesh,
        in_specs=(
            P(("dp", "expert"), None),
            P(),
            P(("dp", "expert"), None),
            P(("dp", "expert"), None),
            P(("dp", "expert"), None, None),
            P(("dp", "expert"), None, None),
            P(("dp", "expert"), None, None),
            P(None, "expert"),
            P(None, "expert"),
            P("dp", "expert"),
            P("dp", "expert"),
        ),
        out_specs=(
            P(("dp", "expert"), None),
            P("dp", "expert"),
            P("dp", "expert"),
            P("dp", "expert"),
            P("dp", "expert"),
        ),
        check_vma=False,
    )
```

```python
import functools
import math

import jax
import jax.numpy as jnp
from jax import lax
from jax.experimental import pallas as pl
from jax.experimental.pallas import tpu as pltpu
from jax.sharding import PartitionSpec as P


LANES = 128


def dispatch_body(ids_ref, tok_ref, gain_ref, out_ref, pos_ref, rows_ref, pos_smem, sem, *, experts, cap):
    top, toks = ids_ref.shape
    width = tok_ref.shape[1]
    sub = width // LANES
    expert_iota = lax.broadcasted_iota(jnp.int32, (experts, toks), 0)
    named = [(ids_ref[k : k + 1, :] == expert_iota).astype(jnp.float32) for k in range(top)]
    total = named[0]
    for k in range(1, top):
        total = total + named[k]
    row = lax.broadcasted_iota(jnp.int32, (toks, toks), 0)
    col = lax.broadcasted_iota(jnp.int32, (toks, toks), 1)
    before = (row < col).astype(jnp.bfloat16)
    earlier = jnp.dot(total.astype(jnp.bfloat16), before, preferred_element_type=jnp.float32)
    for k in range(top):
        slot = jnp.sum(earlier * named[k], axis=0, keepdims=True)
        pos_ref[k : k + 1, :] = ids_ref[k : k + 1, :] * cap + slot.astype(jnp.int32)
    copy = pltpu.make_async_copy(pos_ref, pos_smem, sem)
    copy.start()
    out_ref[...] = jnp.zeros_like(out_ref)
    wide = tok_ref[...].astype(jnp.float32)
    mean_sq = jnp.mean(wide * wide, axis=-1, keepdims=True)
    normed = wide * lax.rsqrt(mean_sq + 1e-06) * gain_ref[...]
    for j in range(sub):
        rows_ref[pl.ds(j, toks, stride=sub), :] = normed[:, j * LANES : (j + 1) * LANES]
    copy.wait()

    def place(t, carry):
        one = rows_ref[pl.ds(pl.multiple_of(t * sub, sub), sub), :].astype(jnp.bfloat16)
        for k in range(top):
            out_ref[pos_smem[k, t]] = one
        return carry

    lax.fori_loop(0, toks, place, 0, unroll=4)


def dispatch(ids, tokens, gain, experts, cap):
    top, toks = ids.shape
    width = tokens.shape[1]
    sub = width // LANES
    return pl.pallas_call(
        functools.partial(dispatch_body, experts=experts, cap=cap),
        name="dispatch",
        out_shape=(
            jax.ShapeDtypeStruct((experts * cap, sub, LANES), jnp.bfloat16),
            jax.ShapeDtypeStruct((top, toks), jnp.int32),
        ),
        scratch_shapes=[
            pltpu.VMEM((toks * sub, LANES), jnp.float32),
            pltpu.SMEM((top, toks), jnp.int32),
            pltpu.SemaphoreType.DMA,
        ],
    )(ids, tokens, gain)


def combine_body(pos_ref, gates_ref, rows_ref, out_ref, even_ref, odd_ref, acc_ref):
    top, toks = pos_ref.shape
    sub = rows_ref.shape[1]

    def gather(t, carry):
        acc = rows_ref[pos_ref[0, t]].astype(jnp.float32) * gates_ref[0, t]
        for k in range(1, top):
            acc = acc + rows_ref[pos_ref[k, t]].astype(jnp.float32) * gates_ref[k, t]
        acc_ref[pl.ds(pl.multiple_of(t * sub, sub), sub), :] = acc
        return carry

    lax.fori_loop(0, toks, gather, 0, unroll=4)
    for j in range(sub):
        block = acc_ref[pl.ds(j, toks, stride=sub), :].astype(jnp.bfloat16)
        out_ref[:, j * LANES : (j + 1) * LANES] = block
        part_ref = (even_ref, odd_ref)[j % 2]
        part_ref[:, j // 2 * LANES : (j // 2 + 1) * LANES] = block


def combine(pos, gates, rows):
    _, toks = pos.shape
    sub = rows.shape[1]
    widths = (sub * LANES, sub // 2 * LANES, sub // 2 * LANES)
    return pl.pallas_call(
        combine_body,
        name="combine",
        grid_spec=pltpu.PrefetchScalarGridSpec(
            num_scalar_prefetch=2,
            grid=(1,),
            in_specs=[pl.BlockSpec(rows.shape, lambda i, p, g: (0, 0, 0), pipeline_mode=pl.Buffered(1))],
            out_specs=tuple(pl.BlockSpec((toks, w), lambda i, p, g: (0, 0)) for w in widths),
            scratch_shapes=[pltpu.VMEM((toks * sub, LANES), jnp.float32)],
        ),
        out_shape=tuple(jax.ShapeDtypeStruct((toks, w), jnp.bfloat16) for w in widths),
    )(pos, gates, rows)


def expert_body(rows_hbm, gate0, up0, down0, gate1, up1, down1, out_hbm,
                rows_ref, x_ref, acc_ref, gate_ref, up_ref, down_ref, hid_ref, in_sem, w_sem, out_sem, *, step, tile, cols):
    count, sub, _ = rows_hbm.shape
    hidden, width = down0.shape
    chunks = count // step
    ins = [
        pltpu.make_async_copy(rows_hbm.at[pl.ds(i * step, step)], rows_ref.at[pl.ds(i * step, step)], in_sem.at[i])
        for i in range(chunks)
    ]
    gates = [pltpu.make_async_copy(w, gate_ref.at[h], w_sem.at[h, 0]) for h, w in enumerate((gate0, gate1))]
    ups = [pltpu.make_async_copy(w, up_ref.at[h], w_sem.at[h, 1]) for h, w in enumerate((up0, up1))]
    downs = [pltpu.make_async_copy(w, down_ref.at[h], w_sem.at[h, 2]) for h, w in enumerate((down0, down1))]
    for c in ins[:2]:
        c.start()
    gates[0].start()
    for c in ins[2:]:
        c.start()
    for c in (ups[0], gates[1], ups[1], downs[0], downs[1]):
        c.start()
    for i in range(chunks):
        ins[i].wait()
        acc_ref[pl.ds(0, step * sub), :] = rows_ref[pl.ds(i * step, step)].astype(jnp.float32).reshape(step * sub, LANES)
        for j in range(sub):
            x_ref[pl.ds(i * step, step), j * LANES : (j + 1) * LANES] = acc_ref[
                pl.ds(j, step, stride=sub), :
            ].astype(jnp.bfloat16)
    contract = (((1,), (1,)), ((), ()))
    for h in range(2):
        gates[h].wait()
        ups[h].wait()
        for lo in range(0, hidden, tile):
            n = min(tile, hidden - lo)
            gate_val = lax.dot_general(x_ref[...], gate_ref[h, pl.ds(lo, n), :], contract, preferred_element_type=jnp.float32)
            up_val = lax.dot_general(x_ref[...], up_ref[h, pl.ds(lo, n), :], contract, preferred_element_type=jnp.float32)
            hid_ref[h, :, lo : lo + n] = (gate_val / (1.0 + jnp.exp(-gate_val)) * up_val).astype(jnp.bfloat16)
    for c in downs:
        c.wait()

    def down_step(d, carry):
        at = pl.ds(pl.multiple_of(d * cols, cols), cols)
        first = jnp.dot(hid_ref[0], down_ref[0, :, at], preferred_element_type=jnp.float32).astype(jnp.bfloat16)
        second = jnp.dot(hid_ref[1], down_ref[1, :, at], preferred_element_type=jnp.float32).astype(jnp.bfloat16)
        both = first.astype(jnp.float32) + second.astype(jnp.float32)
        for j in range(cols // LANES):
            acc_ref[pl.ds(d * (cols // LANES) + j, count, stride=sub), :] = both[:, j * LANES : (j + 1) * LANES]
        return carry

    lax.fori_loop(0, width // cols, down_step, 0)
    outs = [
        pltpu.make_async_copy(rows_ref.at[pl.ds(i * step, step)], out_hbm.at[pl.ds(i * step, step)], out_sem.at[i])
        for i in range(chunks)
    ]
    for i in range(chunks):
        rows_ref[pl.ds(i * step, step)] = (
            acc_ref[pl.ds(i * step * sub, step * sub), :].reshape(step, sub, LANES).astype(jnp.bfloat16)
        )
        outs[i].start()
    for c in outs:
        c.wait()


def expert(rows, gate0, up0, down0, gate1, up1, down1, step=128, tile=256, cols=256):
    count, sub, _ = rows.shape
    hidden, width = down0.shape
    chunks = count // step
    anywhere = pl.BlockSpec(memory_space=pl.ANY)
    return pl.pallas_call(
        functools.partial(expert_body, step=step, tile=tile, cols=cols),
        name="expert",
        in_specs=[anywhere] * 7,
        out_specs=anywhere,
        out_shape=jax.ShapeDtypeStruct(rows.shape, jnp.bfloat16),
        scratch_shapes=[
            pltpu.VMEM(rows.shape, jnp.bfloat16),
            pltpu.VMEM((count, width), jnp.bfloat16),
            pltpu.VMEM((count * sub, LANES), jnp.float32),
            pltpu.VMEM((2, hidden, width), jnp.bfloat16),
            pltpu.VMEM((2, hidden, width), jnp.bfloat16),
            pltpu.VMEM((2, hidden, width), jnp.bfloat16),
            pltpu.VMEM((2, count, hidden), jnp.bfloat16),
            pltpu.SemaphoreType.DMA((chunks,)),
            pltpu.SemaphoreType.DMA((2, 3)),
            pltpu.SemaphoreType.DMA((chunks,)),
        ],
        compiler_params=pltpu.CompilerParams(vmem_limit_bytes=60 * 1024 * 1024),
    )(rows, gate0, up0, down0, gate1, up1, down1)


VMEM_LIMIT = 60 * 1024 * 1024


def terms_body(at_ref, *refs, pieces, scale):
    parts = refs[:pieces]
    cot_hbm, out_hbm, all_rows, rows_ref, cot_ref, cut_ref, sem, side_sem, out_sem = refs[pieces:]
    count = rows_ref.shape[0]
    block = count // (2 * pieces - 4)
    loads = []
    for i, piece in enumerate(parts):
        for k in range(piece.shape[0] // block):
            to = pl.ds(pl.multiple_of(at_ref[2 * i + k], block), block)
            loads.append(pltpu.make_async_copy(piece.at[pl.ds(k * block, block)], rows_ref.at[to], sem.at[2 * i + k]))
    cot_load = pltpu.make_async_copy(cot_hbm, cot_ref, side_sem.at[0])
    cot_load.start()
    for c in loads:
        c.start()
    for c in loads:
        c.wait()
    keep = pltpu.make_async_copy(rows_ref, all_rows, side_sem.at[1])
    keep.start()
    cot_load.wait()
    owners = cut_ref.shape[0]

    def step(d, carry):
        at = pl.ds(pl.multiple_of(d * 2 * LANES, 2 * LANES), 2 * LANES)
        terms = jnp.dot(cot_ref[...], rows_ref[:, at], preferred_element_type=jnp.float32) * scale
        cut_ref[2 * d] = terms[:, :LANES].astype(jnp.bfloat16)
        cut_ref[2 * d + 1] = terms[:, LANES:].astype(jnp.bfloat16)
        pltpu.make_async_copy(cut_ref.at[pl.ds(2 * d, 2)], out_hbm.at[pl.ds(2 * d, 2)], out_sem.at[d]).start()
        return carry

    lax.fori_loop(0, owners // 2, step, 0)
    for d in range(owners // 2):
        pltpu.make_async_copy(cut_ref.at[pl.ds(2 * d, 2)], out_hbm.at[pl.ds(2 * d, 2)], out_sem.at[d]).wait()
    keep.wait()


def features_body(rows0, rows1, one_hbm, two_hbm, feat_one, feat_two, rows_ref, one_ref, two_ref, out_one, out_two, sem, row_sem, out_sem):
    count = rows0.shape[0]
    step = 512
    loads = []
    for half in range(2):
        loads.append(pltpu.make_async_copy(one_hbm.at[:, half], one_ref.at[half], sem.at[half, 0]))
        loads.append(pltpu.make_async_copy(two_hbm.at[:, half], two_ref.at[half], sem.at[half, 1]))
    for c in loads:
        c.start()

    def row_loads(i):
        at = pl.ds(i * step if isinstance(i, int) else pl.multiple_of(i * step, step), step)
        return [
            pltpu.make_async_copy(rows.at[at], rows_ref.at[half, at], row_sem.at[half, i])
            for half, rows in enumerate((rows0, rows1))
        ]

    def stores(i):
        at = pl.ds(i * step if isinstance(i, int) else pl.multiple_of(i * step, step), step)
        return [
            pltpu.make_async_copy(out_one.at[at], feat_one.at[at], out_sem.at[0, i]),
            pltpu.make_async_copy(out_two.at[at], feat_two.at[at], out_sem.at[1, i]),
        ]

    for i in range(count // step):
        for c in row_loads(i):
            c.start()
    for c in loads:
        c.wait()

    def body(i, carry):
        for c in row_loads(i):
            c.wait()
        at = pl.ds(pl.multiple_of(i * step, step), step)
        for w_ref, out_ref in ((one_ref, out_one), (two_ref, out_two)):
            for lo in range(0, w_ref.shape[-1], 256):
                total = [
                    jnp.dot(
                        rows_ref[half, at, :],
                        w_ref[half, :, :, lo : lo + 256].reshape(-1, 256),
                        preferred_element_type=jnp.float32,
                    )
                    for half in range(2)
                ]
                out_ref[at, lo : lo + 256] = (total[0] + total[1]).astype(jnp.bfloat16)
        for c in stores(i):
            c.start()
        return carry

    lax.fori_loop(0, count // step, body, 0)
    for i in range(count // step):
        for c in stores(i):
            c.wait()


def total_of(pieces_ref):
    total = pieces_ref[0].astype(jnp.float32)
    for i in range(1, pieces_ref.shape[0]):
        total = total + pieces_ref[i].astype(jnp.float32)
    return total.T


def sum_first_body(pieces_ref, out_ref):
    out_ref[...] = total_of(pieces_ref)


def sum_last_body(first_ref, pieces_ref, one_ref, two_ref):
    split = one_ref.shape[1]
    half = first_ref.shape[0]
    one_ref[:half] = first_ref[:, :split]
    two_ref[:half] = first_ref[:, split:]
    total = total_of(pieces_ref)
    one_ref[half:] = total[:, :split]
    two_ref[half:] = total[:, split:]


def project(parts, student_one, student_two, cots, move, place):
    rows, half_width = parts[0].shape
    y_hi, x, core = place
    ring, owners = 4, 8
    count = 4 * ring * rows
    split = student_one.shape[1]
    cols = split + student_two.shape[1]
    bf16, f32 = jnp.bfloat16, jnp.float32
    dma = pltpu.SemaphoreType.DMA
    anywhere = pl.BlockSpec(memory_space=pl.ANY)

    def row_of(y, at, c):
        return (y * ring + at % ring) * (2 * rows) + c * rows

    spots = []
    for c in (core, 1 - core):
        for at in (x, x + ring - 1, x + 1):
            spots += [row_of(y_hi, at, c), row_of(1 - y_hi, at, c)]
        spots += [row_of(y_hi, x + 2, c), 0, row_of(1 - y_hi, x + 2, c), 0]
    spots = jnp.stack(spots).astype(jnp.int32)

    def gather(part, other):
        both = jnp.concatenate([part, other], axis=0)
        right = move(both, 0, 1, 0)
        left = move(both, 0, -1, 0)
        far_right = move(right[:rows], 0, 1, 0)
        far_left = move(left[rows:], 0, -1, 0)
        own = [both, right, left, far_right, far_left]
        swapped = []
        for piece in own:
            swapped.append(move(piece, 0, 0, 1))
        return own + swapped

    def terms(pieces):
        return pl.pallas_call(
            functools.partial(terms_body, pieces=len(pieces), scale=1.0 / math.sqrt(count * owners)),
            name="terms",
            grid_spec=pltpu.PrefetchScalarGridSpec(
                num_scalar_prefetch=1,
                grid=(1,),
                in_specs=[anywhere] * (len(pieces) + 1),
                out_specs=(anywhere, anywhere),
                scratch_shapes=[
                    pltpu.VMEM((count, half_width), bf16),
                    pltpu.VMEM((cols, count), bf16),
                    pltpu.VMEM((owners, cols, LANES), bf16),
                    dma((2 * len(pieces),)),
                    dma((2,)),
                    dma((owners // 2,)),
                ],
            ),
            out_shape=(
                jax.ShapeDtypeStruct((owners, cols, LANES), bf16),
                jax.ShapeDtypeStruct((count, half_width), bf16),
            ),
            compiler_params=pltpu.CompilerParams(vmem_limit_bytes=VMEM_LIMIT),
            cost_estimate=pl.CostEstimate(
                flops=2 * count * half_width * cols, transcendentals=0, bytes_accessed=12 << 20
            ),
        )(spots, *pieces, cots)

    other0 = move(parts[0], 2, 0, 0)
    other1 = move(parts[1], 2, 0, 0)
    cut0, rows0 = terms(gather(parts[0], other0))
    cut0 = lax.all_to_all(cut0, "dp", split_axis=0, concat_axis=0, tiled=True)
    cut1, rows1 = terms(gather(parts[1], other1))
    cut1 = lax.all_to_all(cut1, "dp", split_axis=0, concat_axis=0, tiled=True)
    shape = (owners, 2, LANES)
    feat_one, feat_two = pl.pallas_call(
        features_body,
        name="features",
        in_specs=[anywhere] * 4,
        out_specs=(anywhere, anywhere),
        out_shape=(
            jax.ShapeDtypeStruct((count, split), bf16),
            jax.ShapeDtypeStruct((count, cols - split), bf16),
        ),
        scratch_shapes=[
            pltpu.VMEM((2, count, half_width), bf16),
            pltpu.VMEM((2, owners, LANES, split), bf16),
            pltpu.VMEM((2, owners, LANES, cols - split), bf16),
            pltpu.VMEM((count, split), bf16),
            pltpu.VMEM((count, cols - split), bf16),
            dma((2, 2)),
            dma((2, count // 512)),
            dma((2, count // 512)),
        ],
        compiler_params=pltpu.CompilerParams(vmem_limit_bytes=VMEM_LIMIT),
        cost_estimate=pl.CostEstimate(flops=4 * count * half_width * cols, transcendentals=0, bytes_accessed=14 << 20),
    )(rows0, rows1, student_one.reshape(*shape, split), student_two.reshape(*shape, cols - split))
    total0 = pl.pallas_call(
        sum_first_body, name="sum_first", out_shape=jax.ShapeDtypeStruct((LANES, cols), f32)
    )(cut0)
    grad_one, grad_two = pl.pallas_call(
        sum_last_body,
        name="sum_last",
        out_shape=(
            jax.ShapeDtypeStruct((2 * LANES, split), f32),
            jax.ShapeDtypeStruct((2 * LANES, cols - split), f32),
        ),
    )(total0, cut1)
    return feat_one, feat_two, grad_one, grad_two


def local(
    tokens,
    norm_gain,
    expert_ids,
    gate_weights,
    gate_proj,
    up_proj,
    down_proj,
    student_one,
    student_two,
    cot_one,
    cot_two,
):
    tok_dev, model_width = tokens.shape
    top_count = expert_ids.shape[1]
    devices = lax.axis_size("dp") * lax.axis_size("expert")
    experts = devices // 2
    capacity = 2 * ((tok_dev * top_count * 7 + 12 * experts - 1) // (12 * experts))
    sub = model_width // LANES
    axes = ("dp", "expert")
    index = lax.axis_index(axes)

    def move(array, y, x, core):
        def target(d):
            z, y_lo, y_hi, at_x, at_core = d // 32, d // 16 % 2, d // 8 % 2, d // 2 % 4, d % 2
            to_y = (y_hi * 2 + y_lo + y) % 4
            return z * 32 + to_y % 2 * 16 + to_y // 2 * 8 + (at_x + x) % 4 * 2 + (at_core + core) % 2

        return lax.ppermute(array, axes, [(d, target(d)) for d in range(devices)])

    cots = jnp.concatenate([cot_one, cot_two], axis=1).T
    other_gate = move(jnp.swapaxes(gate_proj[0], 0, 1), 0, 0, 1)
    other_up = move(jnp.swapaxes(up_proj[0], 0, 1), 0, 0, 1)
    other_down, cots = lax.optimization_barrier((move(down_proj[0], 0, 0, 1), cots))

    placed, positions = dispatch(expert_ids.T, tokens, norm_gain.reshape(1, -1), experts, capacity)
    received = lax.all_to_all(
        placed.reshape(devices, capacity // 2, sub, LANES),
        ("dp", "expert"),
        split_axis=0,
        concat_axis=0,
        tiled=True,
    )
    expert_out = expert(
        received.reshape(devices * capacity // 2, sub, LANES),
        jnp.swapaxes(gate_proj[0], 0, 1),
        jnp.swapaxes(up_proj[0], 0, 1),
        down_proj[0],
        other_gate,
        other_up,
        other_down,
    )
    returned = lax.all_to_all(
        expert_out.reshape(devices, capacity // 2, sub, LANES),
        ("dp", "expert"),
        split_axis=0,
        concat_axis=0,
        tiled=True,
    )
    layer_out, *parts = combine(positions, gate_weights.T, returned.reshape(experts * capacity, sub, LANES))
    feat_one, feat_two, grad_one, grad_two = project(
        parts, student_one, student_two, cots, move, (index // 8 % 2, index // 2 % 4, index % 2)
    )
    return (layer_out, feat_one, feat_two, grad_one, grad_two)


def solution(mesh):
    return jax.shard_map(
        local,
        mesh=mesh,
        in_specs=(
            P(("dp", "expert"), None),
            P(),
            P(("dp", "expert"), None),
            P(("dp", "expert"), None),
            P(("dp", "expert"), None, None),
            P(("dp", "expert"), None, None),
            P(("dp", "expert"), None, None),
            P(None, "expert"),
            P(None, "expert"),
            P("dp", "expert"),
            P("dp", "expert"),
        ),
        out_specs=(
            P(("dp", "expert"), None),
            P("dp", "expert"),
            P("dp", "expert"),
            P("dp", "expert"),
            P("dp", "expert"),
        ),
        check_vma=False,
    )
```

```python
import functools
import math

import jax
import jax.numpy as jnp
from jax import lax
from jax.experimental import pallas as pl
from jax.experimental.pallas import tpu as pltpu
from jax.sharding import PartitionSpec as P


LANES = 128


def dispatch_body(
    ids_ref, tok_ref, gain_ref, out0, out1, pos_ref, placed_ref, rows_ref, pos_smem, sem, out_sem, *, experts, cap
):
    half = cap // 2
    top, toks = ids_ref.shape
    width = tok_ref.shape[1]
    sub = width // LANES
    expert_iota = lax.broadcasted_iota(jnp.int32, (experts, toks), 0)
    named = [(ids_ref[k : k + 1, :] == expert_iota).astype(jnp.float32) for k in range(top)]
    total = named[0]
    for k in range(1, top):
        total = total + named[k]
    row = lax.broadcasted_iota(jnp.int32, (toks, toks), 0)
    col = lax.broadcasted_iota(jnp.int32, (toks, toks), 1)
    before = (row < col).astype(jnp.bfloat16)
    earlier = jnp.dot(total.astype(jnp.bfloat16), before, preferred_element_type=jnp.float32)
    for k in range(top):
        slot = jnp.sum(earlier * named[k], axis=0, keepdims=True)
        slot = slot.astype(jnp.int32)
        late = (slot >= half).astype(jnp.int32)
        pos_ref[k : k + 1, :] = ids_ref[k : k + 1, :] * half + slot + late * ((experts - 1) * half)
    copy = pltpu.make_async_copy(pos_ref, pos_smem, sem)
    copy.start()
    placed_ref[...] = jnp.zeros_like(placed_ref)
    wide = tok_ref[...].astype(jnp.float32)
    mean_sq = jnp.mean(wide * wide, axis=-1, keepdims=True)
    normed = wide * lax.rsqrt(mean_sq + 1e-06) * gain_ref[...]
    for j in range(sub):
        rows_ref[pl.ds(j, toks, stride=sub), :] = normed[:, j * LANES : (j + 1) * LANES]
    copy.wait()

    def place(t, carry):
        one = rows_ref[pl.ds(pl.multiple_of(t * sub, sub), sub), :].astype(jnp.bfloat16)
        for k in range(top):
            placed_ref[pos_smem[k, t]] = one
        return carry

    lax.fori_loop(0, toks, place, 0, unroll=4)
    chunk = experts * half
    outs = [
        pltpu.make_async_copy(placed_ref.at[pl.ds(i * chunk, chunk)], out, out_sem.at[i])
        for i, out in enumerate((out0, out1))
    ]
    for c in outs:
        c.start()
    for c in outs:
        c.wait()


def dispatch(ids, tokens, gain, experts, cap):
    top, toks = ids.shape
    width = tokens.shape[1]
    sub = width // LANES
    return pl.pallas_call(
        functools.partial(dispatch_body, experts=experts, cap=cap),
        name="dispatch",
        out_shape=(
            jax.ShapeDtypeStruct((experts * (cap // 2), sub, LANES), jnp.bfloat16),
            jax.ShapeDtypeStruct((experts * (cap // 2), sub, LANES), jnp.bfloat16),
            jax.ShapeDtypeStruct((top, toks), jnp.int32),
        ),
        out_specs=(
            pl.BlockSpec(memory_space=pl.ANY),
            pl.BlockSpec(memory_space=pl.ANY),
            pl.BlockSpec(memory_space=pltpu.VMEM),
        ),
        scratch_shapes=[
            pltpu.VMEM((experts * cap, sub, LANES), jnp.bfloat16),
            pltpu.VMEM((toks * sub, LANES), jnp.float32),
            pltpu.SMEM((top, toks), jnp.int32),
            pltpu.SemaphoreType.DMA,
            pltpu.SemaphoreType.DMA((2,)),
        ],
    )(ids, tokens, gain)


def combine_body(pos_ref, gates_ref, rows0_hbm, rows1_hbm, out_ref, even_ref, odd_ref, acc_ref, rows_ref, sem):
    half = rows0_hbm.shape[0]
    loads = [
        pltpu.make_async_copy(rows, rows_ref.at[pl.ds(i * half, half)], sem.at[i])
        for i, rows in enumerate((rows0_hbm, rows1_hbm))
    ]
    for c in loads:
        c.start()
    for c in loads:
        c.wait()
    top, toks = pos_ref.shape
    sub = rows_ref.shape[1]

    def gather(t, carry):
        acc = rows_ref[pos_ref[0, t]].astype(jnp.float32) * gates_ref[0, t]
        for k in range(1, top):
            acc = acc + rows_ref[pos_ref[k, t]].astype(jnp.float32) * gates_ref[k, t]
        acc_ref[pl.ds(pl.multiple_of(t * sub, sub), sub), :] = acc
        return carry

    lax.fori_loop(0, toks, gather, 0, unroll=4)
    for j in range(sub):
        block = acc_ref[pl.ds(j, toks, stride=sub), :].astype(jnp.bfloat16)
        out_ref[:, j * LANES : (j + 1) * LANES] = block
        part_ref = (even_ref, odd_ref)[j % 2]
        part_ref[:, j // 2 * LANES : (j // 2 + 1) * LANES] = block


def combine(pos, gates, rows):
    _, toks = pos.shape
    half, sub, _ = rows[0].shape
    widths = (sub * LANES, sub // 2 * LANES, sub // 2 * LANES)
    return pl.pallas_call(
        combine_body,
        name="combine",
        grid_spec=pltpu.PrefetchScalarGridSpec(
            num_scalar_prefetch=2,
            grid=(1,),
            in_specs=[pl.BlockSpec(memory_space=pl.ANY)] * 2,
            out_specs=tuple(pl.BlockSpec((toks, w), lambda i, p, g: (0, 0)) for w in widths),
            scratch_shapes=[
                pltpu.VMEM((toks * sub, LANES), jnp.float32),
                pltpu.VMEM((2 * half, sub, LANES), jnp.bfloat16),
                pltpu.SemaphoreType.DMA((2,)),
            ],
        ),
        out_shape=tuple(jax.ShapeDtypeStruct((toks, w), jnp.bfloat16) for w in widths),
    )(pos, gates, *rows)


def expert_body(rows_hbm, gate0, up0, down0, gate1, up1, down1, out_hbm,
                rows_ref, x_ref, acc_ref, gate_ref, up_ref, down_ref, hid_ref, in_sem, w_sem, out_sem, *, step, tile, cols):
    count, sub, _ = rows_hbm.shape
    hidden, width = down0.shape
    chunks = count // step
    ins = [
        pltpu.make_async_copy(rows_hbm.at[pl.ds(i * step, step)], rows_ref.at[pl.ds(i * step, step)], in_sem.at[i])
        for i in range(chunks)
    ]
    gates = [pltpu.make_async_copy(w, gate_ref.at[h], w_sem.at[h, 0]) for h, w in enumerate((gate0, gate1))]
    ups = [pltpu.make_async_copy(w, up_ref.at[h], w_sem.at[h, 1]) for h, w in enumerate((up0, up1))]
    downs = [pltpu.make_async_copy(w, down_ref.at[h], w_sem.at[h, 2]) for h, w in enumerate((down0, down1))]
    for c in ins[:2]:
        c.start()
    gates[0].start()
    for c in ins[2:]:
        c.start()
    for c in (ups[0], gates[1], ups[1], downs[0], downs[1]):
        c.start()
    for i in range(chunks):
        ins[i].wait()
        acc_ref[pl.ds(0, step * sub), :] = rows_ref[pl.ds(i * step, step)].astype(jnp.float32).reshape(step * sub, LANES)
        for j in range(sub):
            x_ref[pl.ds(i * step, step), j * LANES : (j + 1) * LANES] = acc_ref[
                pl.ds(j, step, stride=sub), :
            ].astype(jnp.bfloat16)
    contract = (((1,), (1,)), ((), ()))
    for h in range(2):
        gates[h].wait()
        ups[h].wait()
        for lo in range(0, hidden, tile):
            n = min(tile, hidden - lo)
            gate_val = lax.dot_general(x_ref[...], gate_ref[h, pl.ds(lo, n), :], contract, preferred_element_type=jnp.float32)
            up_val = lax.dot_general(x_ref[...], up_ref[h, pl.ds(lo, n), :], contract, preferred_element_type=jnp.float32)
            hid_ref[h, :, lo : lo + n] = (gate_val / (1.0 + jnp.exp(-gate_val)) * up_val).astype(jnp.bfloat16)
    for c in downs:
        c.wait()

    def down_step(d, carry):
        at = pl.ds(pl.multiple_of(d * cols, cols), cols)
        first = jnp.dot(hid_ref[0], down_ref[0, :, at], preferred_element_type=jnp.float32).astype(jnp.bfloat16)
        second = jnp.dot(hid_ref[1], down_ref[1, :, at], preferred_element_type=jnp.float32).astype(jnp.bfloat16)
        both = first.astype(jnp.float32) + second.astype(jnp.float32)
        for j in range(cols // LANES):
            acc_ref[pl.ds(d * (cols // LANES) + j, count, stride=sub), :] = both[:, j * LANES : (j + 1) * LANES]
        return carry

    lax.fori_loop(0, width // cols, down_step, 0)
    outs = [
        pltpu.make_async_copy(rows_ref.at[pl.ds(i * step, step)], out_hbm.at[pl.ds(i * step, step)], out_sem.at[i])
        for i in range(chunks)
    ]
    for i in range(chunks):
        rows_ref[pl.ds(i * step, step)] = (
            acc_ref[pl.ds(i * step * sub, step * sub), :].reshape(step, sub, LANES).astype(jnp.bfloat16)
        )
        outs[i].start()
    for c in outs:
        c.wait()


def expert(rows, gate0, up0, down0, gate1, up1, down1, step=64, tile=256, cols=256):
    count, sub, _ = rows.shape
    hidden, width = down0.shape
    chunks = count // step
    anywhere = pl.BlockSpec(memory_space=pl.ANY)
    return pl.pallas_call(
        functools.partial(expert_body, step=step, tile=tile, cols=cols),
        name="expert",
        in_specs=[anywhere] * 7,
        out_specs=anywhere,
        out_shape=jax.ShapeDtypeStruct(rows.shape, jnp.bfloat16),
        scratch_shapes=[
            pltpu.VMEM(rows.shape, jnp.bfloat16),
            pltpu.VMEM((count, width), jnp.bfloat16),
            pltpu.VMEM((count * sub, LANES), jnp.float32),
            pltpu.VMEM((2, hidden, width), jnp.bfloat16),
            pltpu.VMEM((2, hidden, width), jnp.bfloat16),
            pltpu.VMEM((2, hidden, width), jnp.bfloat16),
            pltpu.VMEM((2, count, hidden), jnp.bfloat16),
            pltpu.SemaphoreType.DMA((chunks,)),
            pltpu.SemaphoreType.DMA((2, 3)),
            pltpu.SemaphoreType.DMA((chunks,)),
        ],
        compiler_params=pltpu.CompilerParams(vmem_limit_bytes=60 * 1024 * 1024),
    )(rows, gate0, up0, down0, gate1, up1, down1)


VMEM_LIMIT = 60 * 1024 * 1024


def terms_body(at_ref, *refs, pieces, scale):
    parts = refs[:pieces]
    cot_hbm, out_hbm, all_rows, rows_ref, cot_ref, cut_ref, sem, side_sem, out_sem = refs[pieces:]
    count = rows_ref.shape[0]
    block = count // (2 * pieces - 4)
    loads = []
    for i, piece in enumerate(parts):
        for k in range(piece.shape[0] // block):
            to = pl.ds(pl.multiple_of(at_ref[2 * i + k], block), block)
            loads.append(pltpu.make_async_copy(piece.at[pl.ds(k * block, block)], rows_ref.at[to], sem.at[2 * i + k]))
    cot_load = pltpu.make_async_copy(cot_hbm, cot_ref, side_sem.at[0])
    cot_load.start()
    for c in loads:
        c.start()
    for c in loads:
        c.wait()
    keep = pltpu.make_async_copy(rows_ref, all_rows, side_sem.at[1])
    keep.start()
    cot_load.wait()
    owners = cut_ref.shape[0]

    def step(d, carry):
        at = pl.ds(pl.multiple_of(d * 2 * LANES, 2 * LANES), 2 * LANES)
        terms = jnp.dot(cot_ref[...], rows_ref[:, at], preferred_element_type=jnp.float32) * scale
        cut_ref[2 * d] = terms[:, :LANES].astype(jnp.bfloat16)
        cut_ref[2 * d + 1] = terms[:, LANES:].astype(jnp.bfloat16)
        pltpu.make_async_copy(cut_ref.at[pl.ds(2 * d, 2)], out_hbm.at[pl.ds(2 * d, 2)], out_sem.at[d]).start()
        return carry

    lax.fori_loop(0, owners // 2, step, 0)
    for d in range(owners // 2):
        pltpu.make_async_copy(cut_ref.at[pl.ds(2 * d, 2)], out_hbm.at[pl.ds(2 * d, 2)], out_sem.at[d]).wait()
    keep.wait()


def features_body(rows0, rows1, one_hbm, two_hbm, feat_one, feat_two, rows_ref, one_ref, two_ref, out_one, out_two, sem, row_sem, out_sem):
    count = rows0.shape[0]
    step = 512
    loads = []
    for half in range(2):
        loads.append(pltpu.make_async_copy(one_hbm.at[:, half], one_ref.at[half], sem.at[half, 0]))
        loads.append(pltpu.make_async_copy(two_hbm.at[:, half], two_ref.at[half], sem.at[half, 1]))
    for c in loads:
        c.start()

    def row_loads(i):
        at = pl.ds(i * step if isinstance(i, int) else pl.multiple_of(i * step, step), step)
        return [
            pltpu.make_async_copy(rows.at[at], rows_ref.at[half, at], row_sem.at[half, i])
            for half, rows in enumerate((rows0, rows1))
        ]

    def stores(i):
        at = pl.ds(i * step if isinstance(i, int) else pl.multiple_of(i * step, step), step)
        return [
            pltpu.make_async_copy(out_one.at[at], feat_one.at[at], out_sem.at[0, i]),
            pltpu.make_async_copy(out_two.at[at], feat_two.at[at], out_sem.at[1, i]),
        ]

    for i in range(count // step):
        for c in row_loads(i):
            c.start()
    for c in loads:
        c.wait()

    def body(i, carry):
        for c in row_loads(i):
            c.wait()
        at = pl.ds(pl.multiple_of(i * step, step), step)
        for w_ref, out_ref in ((one_ref, out_one), (two_ref, out_two)):
            for lo in range(0, w_ref.shape[-1], 256):
                total = [
                    jnp.dot(
                        rows_ref[half, at, :],
                        w_ref[half, :, :, lo : lo + 256].reshape(-1, 256),
                        preferred_element_type=jnp.float32,
                    )
                    for half in range(2)
                ]
                out_ref[at, lo : lo + 256] = (total[0] + total[1]).astype(jnp.bfloat16)
        for c in stores(i):
            c.start()
        return carry

    lax.fori_loop(0, count // step, body, 0)
    for i in range(count // step):
        for c in stores(i):
            c.wait()


def total_of(pieces_ref):
    total = pieces_ref[0].astype(jnp.float32)
    for i in range(1, pieces_ref.shape[0]):
        total = total + pieces_ref[i].astype(jnp.float32)
    return total.T


def sum_first_body(pieces_ref, out_ref):
    out_ref[...] = total_of(pieces_ref)


def sum_last_body(first_ref, pieces_ref, one_ref, two_ref):
    split = one_ref.shape[1]
    half = first_ref.shape[0]
    one_ref[:half] = first_ref[:, :split]
    two_ref[:half] = first_ref[:, split:]
    total = total_of(pieces_ref)
    one_ref[half:] = total[:, :split]
    two_ref[half:] = total[:, split:]


def project(parts, student_one, student_two, cots, move, place):
    rows, half_width = parts[0].shape
    y_hi, x, core = place
    ring, owners = 4, 8
    count = 4 * ring * rows
    split = student_one.shape[1]
    cols = split + student_two.shape[1]
    bf16, f32 = jnp.bfloat16, jnp.float32
    dma = pltpu.SemaphoreType.DMA
    anywhere = pl.BlockSpec(memory_space=pl.ANY)

    def row_of(y, at, c):
        return (y * ring + at % ring) * (2 * rows) + c * rows

    spots = []
    for c in (core, 1 - core):
        for at in (x, x + ring - 1, x + 1):
            spots += [row_of(y_hi, at, c), row_of(1 - y_hi, at, c)]
        spots += [row_of(y_hi, x + 2, c), 0, row_of(1 - y_hi, x + 2, c), 0]
    spots = jnp.stack(spots).astype(jnp.int32)

    def gather(part, other):
        both = jnp.concatenate([part, other], axis=0)
        right = move(both, 0, 1, 0)
        left = move(both, 0, -1, 0)
        far_right = move(right[:rows], 0, 1, 0)
        far_left = move(left[rows:], 0, -1, 0)
        own = [both, right, left, far_right, far_left]
        swapped = []
        for piece in own:
            swapped.append(move(piece, 0, 0, 1))
        return own + swapped

    def terms(pieces):
        return pl.pallas_call(
            functools.partial(terms_body, pieces=len(pieces), scale=1.0 / math.sqrt(count * owners)),
            name="terms",
            grid_spec=pltpu.PrefetchScalarGridSpec(
                num_scalar_prefetch=1,
                grid=(1,),
                in_specs=[anywhere] * (len(pieces) + 1),
                out_specs=(anywhere, anywhere),
                scratch_shapes=[
                    pltpu.VMEM((count, half_width), bf16),
                    pltpu.VMEM((cols, count), bf16),
                    pltpu.VMEM((owners, cols, LANES), bf16),
                    dma((2 * len(pieces),)),
                    dma((2,)),
                    dma((owners // 2,)),
                ],
            ),
            out_shape=(
                jax.ShapeDtypeStruct((owners, cols, LANES), bf16),
                jax.ShapeDtypeStruct((count, half_width), bf16),
            ),
            compiler_params=pltpu.CompilerParams(vmem_limit_bytes=VMEM_LIMIT),
            cost_estimate=pl.CostEstimate(
                flops=2 * count * half_width * cols, transcendentals=0, bytes_accessed=12 << 20
            ),
        )(spots, *pieces, cots)

    other0 = move(parts[0], 2, 0, 0)
    other1 = move(parts[1], 2, 0, 0)
    cut0, rows0 = terms(gather(parts[0], other0))
    cut0 = lax.all_to_all(cut0, "dp", split_axis=0, concat_axis=0, tiled=True)
    cut1, rows1 = terms(gather(parts[1], other1))
    cut1 = lax.all_to_all(cut1, "dp", split_axis=0, concat_axis=0, tiled=True)
    shape = (owners, 2, LANES)
    feat_one, feat_two = pl.pallas_call(
        features_body,
        name="features",
        in_specs=[anywhere] * 4,
        out_specs=(anywhere, anywhere),
        out_shape=(
            jax.ShapeDtypeStruct((count, split), bf16),
            jax.ShapeDtypeStruct((count, cols - split), bf16),
        ),
        scratch_shapes=[
            pltpu.VMEM((2, count, half_width), bf16),
            pltpu.VMEM((2, owners, LANES, split), bf16),
            pltpu.VMEM((2, owners, LANES, cols - split), bf16),
            pltpu.VMEM((count, split), bf16),
            pltpu.VMEM((count, cols - split), bf16),
            dma((2, 2)),
            dma((2, count // 512)),
            dma((2, count // 512)),
        ],
        compiler_params=pltpu.CompilerParams(vmem_limit_bytes=VMEM_LIMIT),
        cost_estimate=pl.CostEstimate(flops=4 * count * half_width * cols, transcendentals=0, bytes_accessed=14 << 20),
    )(rows0, rows1, student_one.reshape(*shape, split), student_two.reshape(*shape, cols - split))
    total0 = pl.pallas_call(
        sum_first_body, name="sum_first", out_shape=jax.ShapeDtypeStruct((LANES, cols), f32)
    )(cut0)
    grad_one, grad_two = pl.pallas_call(
        sum_last_body,
        name="sum_last",
        out_shape=(
            jax.ShapeDtypeStruct((2 * LANES, split), f32),
            jax.ShapeDtypeStruct((2 * LANES, cols - split), f32),
        ),
    )(total0, cut1)
    return feat_one, feat_two, grad_one, grad_two


def local(
    tokens,
    norm_gain,
    expert_ids,
    gate_weights,
    gate_proj,
    up_proj,
    down_proj,
    student_one,
    student_two,
    cot_one,
    cot_two,
):
    tok_dev, model_width = tokens.shape
    top_count = expert_ids.shape[1]
    axes = ("dp", "pair", "core")
    devices = lax.axis_size(axes)
    experts = devices // 2
    capacity = 2 * ((tok_dev * top_count * 7 + 12 * experts - 1) // (12 * experts))
    sub = model_width // LANES
    index = lax.axis_index(axes)

    def move(array, y, x, core):
        def target(d):
            z, y_lo, y_hi, at_x, at_core = d // 32, d // 16 % 2, d // 8 % 2, d // 2 % 4, d % 2
            to_y = (y_hi * 2 + y_lo + y) % 4
            return z * 32 + to_y % 2 * 16 + to_y // 2 * 8 + (at_x + x) % 4 * 2 + (at_core + core) % 2

        return lax.ppermute(array, axes, [(d, target(d)) for d in range(devices)])

    cots = jnp.concatenate([cot_one, cot_two], axis=1).T
    other_gate = move(jnp.swapaxes(gate_proj[0], 0, 1), 0, 0, 1)
    other_up = move(jnp.swapaxes(up_proj[0], 0, 1), 0, 0, 1)
    other_down, cots = lax.optimization_barrier((move(down_proj[0], 0, 0, 1), cots))

    *placed, positions = dispatch(expert_ids.T, tokens, norm_gain.reshape(1, -1), experts, capacity)
    chunks = [c.reshape(experts, capacity // 2, sub, LANES) for c in placed]

    def exchange(rows):
        return lax.all_to_all(rows, ("dp", "pair"), split_axis=0, concat_axis=0, tiled=True)

    weights = (
        jnp.swapaxes(gate_proj[0], 0, 1),
        jnp.swapaxes(up_proj[0], 0, 1),
        down_proj[0],
        other_gate,
        other_up,
        other_down,
    )

    def run(rows):
        out = expert(rows.reshape(experts * (capacity // 2), sub, LANES), *weights)
        return out.reshape(experts, capacity // 2, sub, LANES)

    sent = [exchange(chunks[c]) for c in range(2)]
    done = [run(sent[c]) for c in range(2)]
    back = [exchange(done[c]).reshape(-1, sub, LANES) for c in range(2)]
    layer_out, *parts = combine(positions, gate_weights.T, back)
    feat_one, feat_two, grad_one, grad_two = project(
        parts, student_one, student_two, cots, move, (index // 8 % 2, index // 2 % 4, index % 2)
    )
    return (layer_out, feat_one, feat_two, grad_one, grad_two)


def solution(mesh):
    batches, group = mesh.devices.shape
    split = jax.sharding.Mesh(mesh.devices.reshape(batches, group // 2, 2), ("dp", "pair", "core"))
    group, whole = ("pair", "core"), ("dp", "pair", "core")
    return jax.shard_map(
        local,
        mesh=split,
        in_specs=(
            P(whole, None),
            P(),
            P(whole, None),
            P(whole, None),
            P(whole, None, None),
            P(whole, None, None),
            P(whole, None, None),
            P(None, group),
            P(None, group),
            P("dp", group),
            P("dp", group),
        ),
        out_specs=(
            P(whole, None),
            P("dp", group),
            P("dp", group),
            P("dp", group),
            P("dp", group),
        ),
        check_vma=False,
    )
```

```python
import functools
import math

import jax
import jax.numpy as jnp
from jax import lax
from jax.experimental import pallas as pl
from jax.experimental.pallas import tpu as pltpu
from jax.sharding import PartitionSpec as P


LANES = 128


def dispatch_body(ids_ref, tok_ref, gain_ref, out_ref, pos_ref, rows_ref, pos_smem, sem, *, experts, cap):
    top, toks = ids_ref.shape
    width = tok_ref.shape[1]
    sub = width // LANES
    expert_iota = lax.broadcasted_iota(jnp.int32, (experts, toks), 0)
    named = [(ids_ref[k : k + 1, :] == expert_iota).astype(jnp.float32) for k in range(top)]
    total = named[0]
    for k in range(1, top):
        total = total + named[k]
    row = lax.broadcasted_iota(jnp.int32, (toks, toks), 0)
    col = lax.broadcasted_iota(jnp.int32, (toks, toks), 1)
    before = (row < col).astype(jnp.bfloat16)
    earlier = jnp.dot(total.astype(jnp.bfloat16), before, preferred_element_type=jnp.float32)
    for k in range(top):
        slot = jnp.sum(earlier * named[k], axis=0, keepdims=True)
        pos_ref[k : k + 1, :] = ids_ref[k : k + 1, :] * cap + slot.astype(jnp.int32)
    copy = pltpu.make_async_copy(pos_ref, pos_smem, sem)
    copy.start()
    out_ref[...] = jnp.zeros_like(out_ref)
    wide = tok_ref[...].astype(jnp.float32)
    mean_sq = jnp.mean(wide * wide, axis=-1, keepdims=True)
    normed = wide * lax.rsqrt(mean_sq + 1e-06) * gain_ref[...]
    for j in range(sub):
        rows_ref[pl.ds(j, toks, stride=sub), :] = normed[:, j * LANES : (j + 1) * LANES]
    copy.wait()

    def place(t, carry):
        one = rows_ref[pl.ds(pl.multiple_of(t * sub, sub), sub), :].astype(jnp.bfloat16)
        for k in range(top):
            out_ref[pos_smem[k, t]] = one
        return carry

    lax.fori_loop(0, toks, place, 0, unroll=4)


def dispatch(ids, tokens, gain, experts, cap):
    top, toks = ids.shape
    width = tokens.shape[1]
    sub = width // LANES
    return pl.pallas_call(
        functools.partial(dispatch_body, experts=experts, cap=cap),
        name="dispatch",
        out_shape=(
            jax.ShapeDtypeStruct((experts * cap, sub, LANES), jnp.bfloat16),
            jax.ShapeDtypeStruct((top, toks), jnp.int32),
        ),
        scratch_shapes=[
            pltpu.VMEM((toks * sub, LANES), jnp.float32),
            pltpu.SMEM((top, toks), jnp.int32),
            pltpu.SemaphoreType.DMA,
        ],
    )(ids, tokens, gain)


def combine_body(pos_ref, gates_ref, rows_ref, out_ref, even_ref, odd_ref, acc_ref):
    top, toks = pos_ref.shape
    sub = rows_ref.shape[1]

    def gather(t, carry):
        acc = rows_ref[pos_ref[0, t]].astype(jnp.float32) * gates_ref[0, t]
        for k in range(1, top):
            acc = acc + rows_ref[pos_ref[k, t]].astype(jnp.float32) * gates_ref[k, t]
        acc_ref[pl.ds(pl.multiple_of(t * sub, sub), sub), :] = acc
        return carry

    lax.fori_loop(0, toks, gather, 0, unroll=4)
    for j in range(sub):
        block = acc_ref[pl.ds(j, toks, stride=sub), :].astype(jnp.bfloat16)
        out_ref[:, j * LANES : (j + 1) * LANES] = block
        part_ref = (even_ref, odd_ref)[j % 2]
        part_ref[:, j // 2 * LANES : (j // 2 + 1) * LANES] = block


def combine(pos, gates, rows):
    _, toks = pos.shape
    sub = rows.shape[1]
    widths = (sub * LANES, sub // 2 * LANES, sub // 2 * LANES)
    return pl.pallas_call(
        combine_body,
        name="combine",
        grid_spec=pltpu.PrefetchScalarGridSpec(
            num_scalar_prefetch=2,
            grid=(1,),
            in_specs=[pl.BlockSpec(rows.shape, lambda i, p, g: (0, 0, 0), pipeline_mode=pl.Buffered(1))],
            out_specs=tuple(pl.BlockSpec((toks, w), lambda i, p, g: (0, 0)) for w in widths),
            scratch_shapes=[pltpu.VMEM((toks * sub, LANES), jnp.float32)],
        ),
        out_shape=tuple(jax.ShapeDtypeStruct((toks, w), jnp.bfloat16) for w in widths),
    )(pos, gates, rows)


def expert_body(rows_hbm, gate0, up0, down0, gate1, up1, down1, out_hbm,
                rows_ref, x_ref, acc_ref, gate_ref, up_ref, down_ref, hid_ref, in_sem, w_sem, out_sem, *, step, tile, cols):
    count, sub, _ = rows_hbm.shape
    hidden, width = down0.shape
    chunks = count // step
    ins = [
        pltpu.make_async_copy(rows_hbm.at[pl.ds(i * step, step)], rows_ref.at[pl.ds(i * step, step)], in_sem.at[i])
        for i in range(chunks)
    ]
    gates = [pltpu.make_async_copy(w, gate_ref.at[h], w_sem.at[h, 0]) for h, w in enumerate((gate0, gate1))]
    ups = [pltpu.make_async_copy(w, up_ref.at[h], w_sem.at[h, 1]) for h, w in enumerate((up0, up1))]
    downs = [pltpu.make_async_copy(w, down_ref.at[h], w_sem.at[h, 2]) for h, w in enumerate((down0, down1))]
    for c in ins[:2]:
        c.start()
    gates[0].start()
    for c in ins[2:]:
        c.start()
    for c in (ups[0], gates[1], ups[1], downs[0], downs[1]):
        c.start()
    for i in range(chunks):
        ins[i].wait()
        acc_ref[pl.ds(0, step * sub), :] = rows_ref[pl.ds(i * step, step)].astype(jnp.float32).reshape(step * sub, LANES)
        for j in range(sub):
            x_ref[pl.ds(i * step, step), j * LANES : (j + 1) * LANES] = acc_ref[
                pl.ds(j, step, stride=sub), :
            ].astype(jnp.bfloat16)
    contract = (((1,), (1,)), ((), ()))
    for h in range(2):
        gates[h].wait()
        ups[h].wait()
        for lo in range(0, hidden, tile):
            n = min(tile, hidden - lo)
            gate_val = lax.dot_general(x_ref[...], gate_ref[h, pl.ds(lo, n), :], contract, preferred_element_type=jnp.float32)
            up_val = lax.dot_general(x_ref[...], up_ref[h, pl.ds(lo, n), :], contract, preferred_element_type=jnp.float32)
            hid_ref[h, :, lo : lo + n] = (0.5 * gate_val * (1.0 + jnp.tanh(0.5 * gate_val)) * up_val).astype(jnp.bfloat16)
    for c in downs:
        c.wait()

    def down_step(d, carry):
        at = pl.ds(pl.multiple_of(d * cols, cols), cols)
        first = jnp.dot(hid_ref[0], down_ref[0, :, at], preferred_element_type=jnp.float32).astype(jnp.bfloat16)
        second = jnp.dot(hid_ref[1], down_ref[1, :, at], preferred_element_type=jnp.float32).astype(jnp.bfloat16)
        both = first.astype(jnp.float32) + second.astype(jnp.float32)
        for j in range(cols // LANES):
            acc_ref[pl.ds(d * (cols // LANES) + j, count, stride=sub), :] = both[:, j * LANES : (j + 1) * LANES]
        return carry

    lax.fori_loop(0, width // cols, down_step, 0)
    outs = [
        pltpu.make_async_copy(rows_ref.at[pl.ds(i * step, step)], out_hbm.at[pl.ds(i * step, step)], out_sem.at[i])
        for i in range(chunks)
    ]
    for i in range(chunks):
        rows_ref[pl.ds(i * step, step)] = (
            acc_ref[pl.ds(i * step * sub, step * sub), :].reshape(step, sub, LANES).astype(jnp.bfloat16)
        )
        outs[i].start()
    for c in outs:
        c.wait()


def expert(rows, gate0, up0, down0, gate1, up1, down1, step=128, tile=256, cols=256):
    count, sub, _ = rows.shape
    hidden, width = down0.shape
    chunks = count // step
    anywhere = pl.BlockSpec(memory_space=pl.ANY)
    return pl.pallas_call(
        functools.partial(expert_body, step=step, tile=tile, cols=cols),
        name="expert",
        in_specs=[anywhere] * 7,
        out_specs=anywhere,
        out_shape=jax.ShapeDtypeStruct(rows.shape, jnp.bfloat16),
        scratch_shapes=[
            pltpu.VMEM(rows.shape, jnp.bfloat16),
            pltpu.VMEM((count, width), jnp.bfloat16),
            pltpu.VMEM((count * sub, LANES), jnp.float32),
            pltpu.VMEM((2, hidden, width), jnp.bfloat16),
            pltpu.VMEM((2, hidden, width), jnp.bfloat16),
            pltpu.VMEM((2, hidden, width), jnp.bfloat16),
            pltpu.VMEM((2, count, hidden), jnp.bfloat16),
            pltpu.SemaphoreType.DMA((chunks,)),
            pltpu.SemaphoreType.DMA((2, 3)),
            pltpu.SemaphoreType.DMA((chunks,)),
        ],
        compiler_params=pltpu.CompilerParams(vmem_limit_bytes=60 * 1024 * 1024),
    )(rows, gate0, up0, down0, gate1, up1, down1)


VMEM_LIMIT = 60 * 1024 * 1024


def terms_body(at_ref, *refs, pieces, blocks, scale):
    parts = refs[:pieces]
    cot_hbm, out_hbm, all_rows, rows_ref, cot_ref, cut_ref, sem, side_sem, out_sem = refs[pieces:]
    loads = []
    for i, (piece, start, size) in enumerate(blocks):
        to = pl.ds(pl.multiple_of(at_ref[i], size), size)
        loads.append(pltpu.make_async_copy(parts[piece].at[pl.ds(start, size)], rows_ref.at[to], sem.at[i]))
    cot_load = pltpu.make_async_copy(cot_hbm, cot_ref, side_sem.at[0])
    cot_load.start()
    for c in loads:
        c.start()
    for c in loads:
        c.wait()
    keep = pltpu.make_async_copy(rows_ref, all_rows, side_sem.at[1])
    keep.start()
    cot_load.wait()
    owners = cut_ref.shape[0]

    def step(d, carry):
        at = pl.ds(pl.multiple_of(d * 2 * LANES, 2 * LANES), 2 * LANES)
        terms = jnp.dot(cot_ref[...], rows_ref[:, at], preferred_element_type=jnp.float32) * scale
        cut_ref[2 * d] = terms[:, :LANES].astype(jnp.bfloat16)
        cut_ref[2 * d + 1] = terms[:, LANES:].astype(jnp.bfloat16)
        pltpu.make_async_copy(cut_ref.at[pl.ds(2 * d, 2)], out_hbm.at[pl.ds(2 * d, 2)], out_sem.at[d]).start()
        return carry

    lax.fori_loop(0, owners // 2, step, 0)
    for d in range(owners // 2):
        pltpu.make_async_copy(cut_ref.at[pl.ds(2 * d, 2)], out_hbm.at[pl.ds(2 * d, 2)], out_sem.at[d]).wait()
    keep.wait()


def features_body(rows0, rows1, one_hbm, two_hbm, feat_one, feat_two, rows_ref, one_ref, two_ref, out_one, out_two, sem, row_sem, out_sem):
    count = rows0.shape[0]
    step = 512
    loads = []
    for half in range(2):
        loads.append(pltpu.make_async_copy(one_hbm.at[:, half], one_ref.at[half], sem.at[half, 0]))
        loads.append(pltpu.make_async_copy(two_hbm.at[:, half], two_ref.at[half], sem.at[half, 1]))
    for c in loads:
        c.start()

    def row_loads(i):
        at = pl.ds(i * step if isinstance(i, int) else pl.multiple_of(i * step, step), step)
        return [
            pltpu.make_async_copy(rows.at[at], rows_ref.at[half, at], row_sem.at[half, i])
            for half, rows in enumerate((rows0, rows1))
        ]

    def stores(i):
        at = pl.ds(i * step if isinstance(i, int) else pl.multiple_of(i * step, step), step)
        return [
            pltpu.make_async_copy(out_one.at[at], feat_one.at[at], out_sem.at[0, i]),
            pltpu.make_async_copy(out_two.at[at], feat_two.at[at], out_sem.at[1, i]),
        ]

    for i in range(count // step):
        for c in row_loads(i):
            c.start()
    for c in loads:
        c.wait()

    def body(i, carry):
        for c in row_loads(i):
            c.wait()
        at = pl.ds(pl.multiple_of(i * step, step), step)
        for w_ref, out_ref in ((one_ref, out_one), (two_ref, out_two)):
            for lo in range(0, w_ref.shape[-1], 256):
                total = [
                    jnp.dot(
                        rows_ref[half, at, :],
                        w_ref[half, :, :, lo : lo + 256].reshape(-1, 256),
                        preferred_element_type=jnp.float32,
                    )
                    for half in range(2)
                ]
                out_ref[at, lo : lo + 256] = (total[0] + total[1]).astype(jnp.bfloat16)
        for c in stores(i):
            c.start()
        return carry

    lax.fori_loop(0, count // step, body, 0)
    for i in range(count // step):
        for c in stores(i):
            c.wait()


def total_of(pieces_ref):
    total = pieces_ref[0].astype(jnp.float32)
    for i in range(1, pieces_ref.shape[0]):
        total = total + pieces_ref[i].astype(jnp.float32)
    return total.T


def sum_first_body(pieces_ref, out_ref):
    out_ref[...] = total_of(pieces_ref)


def sum_last_body(first_ref, pieces_ref, one_ref, two_ref):
    split = one_ref.shape[1]
    half = first_ref.shape[0]
    one_ref[:half] = first_ref[:, :split]
    two_ref[:half] = first_ref[:, split:]
    total = total_of(pieces_ref)
    one_ref[half:] = total[:, :split]
    two_ref[half:] = total[:, split:]


def project(parts, student_one, student_two, cots, move, place):
    rows, half_width = parts[0].shape
    y_hi, x, core = place
    ring, owners = 4, 8
    count = 4 * ring * rows
    split = student_one.shape[1]
    cols = split + student_two.shape[1]
    bf16, f32 = jnp.bfloat16, jnp.float32
    dma = pltpu.SemaphoreType.DMA
    anywhere = pl.BlockSpec(memory_space=pl.ANY)
    inside = pl.BlockSpec(memory_space=pltpu.VMEM)

    def row_of(y, at, c):
        return (y * ring + at % ring) * (2 * rows) + c * rows

    def spread(y, c):
        half = rows // 2
        near = [(0, rows, row_of(y, x + d, c)) for d in (0, ring - 1, 1)]
        return near + [(0, half, row_of(y, x + 2, c) + k * half) for k in range(2)]

    def gather(block):
        half = block.shape[0] // 2
        right = move(block, 0, 1, 0)
        left = move(block, 0, -1, 0)
        far_right = move(right[:half], 0, 1, 0)
        far_left = move(left[half:], 0, -1, 0)
        own = [block, right, left, far_right, far_left]
        swapped = []
        for piece in own:
            swapped.append(move(piece, 0, 0, 1))
        return own + swapped

    def single(y, first):
        return [(first + i, *spot) for i, spot in enumerate(spread(y, core) + spread(y, 1 - core))]

    def double(first):
        out = []
        for k, c in enumerate((core, 1 - core)):
            at = first + 5 * k
            for side, y in enumerate((y_hi, 1 - y_hi)):
                out += [(at + i, side * rows, rows, row_of(y, x + d, c)) for i, d in enumerate((0, ring - 1, 1))]
                out.append((at + 3 + side, 0, rows, row_of(y, x + 2, c)))
        return out

    def terms(pieces, spots):
        blocks = tuple(spot[:3] for spot in spots)
        return pl.pallas_call(
            functools.partial(
                terms_body, pieces=len(pieces), blocks=blocks, scale=1.0 / math.sqrt(count * owners)
            ),
            name="terms",
            grid_spec=pltpu.PrefetchScalarGridSpec(
                num_scalar_prefetch=1,
                grid=(1,),
                in_specs=[anywhere] * (len(pieces) + 1),
                out_specs=(anywhere, anywhere),
                scratch_shapes=[
                    pltpu.VMEM((count, half_width), bf16),
                    pltpu.VMEM((cols, count), bf16),
                    pltpu.VMEM((owners, cols, LANES), bf16),
                    dma((len(blocks),)),
                    dma((2,)),
                    dma((owners // 2,)),
                ],
            ),
            out_shape=(
                jax.ShapeDtypeStruct((owners, cols, LANES), bf16),
                jax.ShapeDtypeStruct((count, half_width), bf16),
            ),
            compiler_params=pltpu.CompilerParams(vmem_limit_bytes=VMEM_LIMIT),
            cost_estimate=pl.CostEstimate(
                flops=2 * count * half_width * cols, transcendentals=0, bytes_accessed=12 << 20
            ),
        )(jnp.stack([spot[3] for spot in spots]).astype(jnp.int32), *pieces, cots)

    other0 = move(parts[0], 2, 0, 0)
    other1 = move(parts[1], 2, 0, 0)
    cut0, rows0 = terms(gather(parts[0]) + gather(other0), single(y_hi, 0) + single(1 - y_hi, 10))
    cut0 = lax.all_to_all(cut0, "dp", split_axis=0, concat_axis=0, tiled=True)
    cut1, rows1 = terms(gather(jnp.concatenate([parts[1], other1], axis=0)), double(0))
    cut1 = lax.all_to_all(cut1, "dp", split_axis=0, concat_axis=0, tiled=True)
    shape = (owners, 2, LANES)
    feat_one, feat_two = pl.pallas_call(
        features_body,
        name="features",
        in_specs=[anywhere] * 4,
        out_specs=(anywhere, anywhere),
        out_shape=(
            jax.ShapeDtypeStruct((count, split), bf16),
            jax.ShapeDtypeStruct((count, cols - split), bf16),
        ),
        scratch_shapes=[
            pltpu.VMEM((2, count, half_width), bf16),
            pltpu.VMEM((2, owners, LANES, split), bf16),
            pltpu.VMEM((2, owners, LANES, cols - split), bf16),
            pltpu.VMEM((count, split), bf16),
            pltpu.VMEM((count, cols - split), bf16),
            dma((2, 2)),
            dma((2, count // 512)),
            dma((2, count // 512)),
        ],
        compiler_params=pltpu.CompilerParams(vmem_limit_bytes=VMEM_LIMIT),
        cost_estimate=pl.CostEstimate(flops=4 * count * half_width * cols, transcendentals=0, bytes_accessed=14 << 20),
    )(rows0, rows1, student_one.reshape(*shape, split), student_two.reshape(*shape, cols - split))
    total0 = pl.pallas_call(
        sum_first_body,
        name="sum_first",
        in_specs=[inside],
        out_specs=inside,
        out_shape=jax.ShapeDtypeStruct((LANES, cols), f32),
    )(cut0)
    grad_one, grad_two = pl.pallas_call(
        sum_last_body,
        name="sum_last",
        in_specs=[inside, inside],
        out_specs=(inside, inside),
        out_shape=(
            jax.ShapeDtypeStruct((2 * LANES, split), f32),
            jax.ShapeDtypeStruct((2 * LANES, cols - split), f32),
        ),
    )(total0, cut1)
    return feat_one, feat_two, grad_one, grad_two


def local(
    tokens,
    norm_gain,
    expert_ids,
    gate_weights,
    gate_proj,
    up_proj,
    down_proj,
    student_one,
    student_two,
    cot_one,
    cot_two,
):
    tok_dev, model_width = tokens.shape
    top_count = expert_ids.shape[1]
    devices = lax.axis_size("dp") * lax.axis_size("expert")
    experts = devices // 2
    capacity = 2 * ((tok_dev * top_count * 7 + 12 * experts - 1) // (12 * experts))
    sub = model_width // LANES
    axes = ("dp", "expert")
    index = lax.axis_index(axes)

    def move(array, y, x, core):
        def target(d):
            z, y_lo, y_hi, at_x, at_core = d // 32, d // 16 % 2, d // 8 % 2, d // 2 % 4, d % 2
            to_y = (y_hi * 2 + y_lo + y) % 4
            return z * 32 + to_y % 2 * 16 + to_y // 2 * 8 + (at_x + x) % 4 * 2 + (at_core + core) % 2

        return lax.ppermute(array, axes, [(d, target(d)) for d in range(devices)])

    cots = jnp.concatenate([cot_one, cot_two], axis=1).T
    other_gate = move(jnp.swapaxes(gate_proj[0], 0, 1), 0, 0, 1)
    other_up = move(jnp.swapaxes(up_proj[0], 0, 1), 0, 0, 1)
    other_down, cots = lax.optimization_barrier((move(down_proj[0], 0, 0, 1), cots))

    placed, positions = dispatch(expert_ids.T, tokens, norm_gain.reshape(1, -1), experts, capacity)
    received = lax.all_to_all(
        placed.reshape(devices, capacity // 2, sub, LANES),
        ("dp", "expert"),
        split_axis=0,
        concat_axis=0,
        tiled=True,
    )
    expert_out = expert(
        received.reshape(devices * capacity // 2, sub, LANES),
        jnp.swapaxes(gate_proj[0], 0, 1),
        jnp.swapaxes(up_proj[0], 0, 1),
        down_proj[0],
        other_gate,
        other_up,
        other_down,
    )
    returned = lax.all_to_all(
        expert_out.reshape(devices, capacity // 2, sub, LANES),
        ("dp", "expert"),
        split_axis=0,
        concat_axis=0,
        tiled=True,
    )
    layer_out, *parts = combine(positions, gate_weights.T, returned.reshape(experts * capacity, sub, LANES))
    feat_one, feat_two, grad_one, grad_two = project(
        parts, student_one, student_two, cots, move, (index // 8 % 2, index // 2 % 4, index % 2)
    )
    return (layer_out, feat_one, feat_two, grad_one, grad_two)


def solution(mesh):
    return jax.shard_map(
        local,
        mesh=mesh,
        in_specs=(
            P(("dp", "expert"), None),
            P(),
            P(("dp", "expert"), None),
            P(("dp", "expert"), None),
            P(("dp", "expert"), None, None),
            P(("dp", "expert"), None, None),
            P(("dp", "expert"), None, None),
            P(None, "expert"),
            P(None, "expert"),
            P("dp", "expert"),
            P("dp", "expert"),
        ),
        out_specs=(
            P(("dp", "expert"), None),
            P("dp", "expert"),
            P("dp", "expert"),
            P("dp", "expert"),
            P("dp", "expert"),
        ),
        check_vma=False,
    )
```

```python
import functools
import math

import jax
import jax.numpy as jnp
from jax import lax
from jax.experimental import pallas as pl
from jax.experimental.pallas import tpu as pltpu
from jax.sharding import PartitionSpec as P


LANES = 128


def dispatch_body(ids_ref, tok_ref, gain_ref, out_ref, pos_ref, rows_ref, pos_smem, sem, *, experts, cap):
    top, toks = ids_ref.shape
    width = tok_ref.shape[1]
    sub = width // LANES
    expert_iota = lax.broadcasted_iota(jnp.int32, (experts, toks), 0)
    named = [(ids_ref[k : k + 1, :] == expert_iota).astype(jnp.float32) for k in range(top)]
    total = named[0]
    for k in range(1, top):
        total = total + named[k]
    row = lax.broadcasted_iota(jnp.int32, (toks, toks), 0)
    col = lax.broadcasted_iota(jnp.int32, (toks, toks), 1)
    before = (row < col).astype(jnp.bfloat16)
    earlier = jnp.dot(total.astype(jnp.bfloat16), before, preferred_element_type=jnp.float32)
    for k in range(top):
        slot = jnp.sum(earlier * named[k], axis=0, keepdims=True)
        pos_ref[k : k + 1, :] = ids_ref[k : k + 1, :] * cap + slot.astype(jnp.int32)
    copy = pltpu.make_async_copy(pos_ref, pos_smem, sem)
    copy.start()
    out_ref[...] = jnp.zeros_like(out_ref)
    wide = tok_ref[...].astype(jnp.float32)
    mean_sq = jnp.mean(wide * wide, axis=-1, keepdims=True)
    normed = wide * lax.rsqrt(mean_sq + 1e-06) * gain_ref[...]
    for j in range(sub):
        rows_ref[pl.ds(j, toks, stride=sub), :] = normed[:, j * LANES : (j + 1) * LANES]
    copy.wait()

    def place(t, carry):
        one = rows_ref[pl.ds(pl.multiple_of(t * sub, sub), sub), :].astype(jnp.bfloat16)
        for k in range(top):
            out_ref[pos_smem[k, t]] = one
        return carry

    lax.fori_loop(0, toks, place, 0, unroll=4)


def dispatch(ids, tokens, gain, experts, cap):
    top, toks = ids.shape
    width = tokens.shape[1]
    sub = width // LANES
    return pl.pallas_call(
        functools.partial(dispatch_body, experts=experts, cap=cap),
        name="dispatch",
        out_shape=(
            jax.ShapeDtypeStruct((experts * cap, sub, LANES), jnp.bfloat16),
            jax.ShapeDtypeStruct((top, toks), jnp.int32),
        ),
        scratch_shapes=[
            pltpu.VMEM((toks * sub, LANES), jnp.float32),
            pltpu.SMEM((top, toks), jnp.int32),
            pltpu.SemaphoreType.DMA,
        ],
    )(ids, tokens, gain)


def combine_body(pos_ref, gates_ref, rows_ref, out_ref, even_ref, odd_ref, acc_ref):
    top, toks = pos_ref.shape
    sub = rows_ref.shape[1]

    def gather(t, carry):
        acc = rows_ref[pos_ref[0, t]].astype(jnp.float32) * gates_ref[0, t]
        for k in range(1, top):
            acc = acc + rows_ref[pos_ref[k, t]].astype(jnp.float32) * gates_ref[k, t]
        acc_ref[pl.ds(pl.multiple_of(t * sub, sub), sub), :] = acc
        return carry

    lax.fori_loop(0, toks, gather, 0, unroll=4)
    for j in range(sub):
        block = acc_ref[pl.ds(j, toks, stride=sub), :].astype(jnp.bfloat16)
        out_ref[:, j * LANES : (j + 1) * LANES] = block
        part_ref = (even_ref, odd_ref)[j % 2]
        part_ref[:, j // 2 * LANES : (j // 2 + 1) * LANES] = block


def combine(pos, gates, rows):
    _, toks = pos.shape
    sub = rows.shape[1]
    widths = (sub * LANES, sub // 2 * LANES, sub // 2 * LANES)
    return pl.pallas_call(
        combine_body,
        name="combine",
        grid_spec=pltpu.PrefetchScalarGridSpec(
            num_scalar_prefetch=2,
            grid=(1,),
            in_specs=[pl.BlockSpec(rows.shape, lambda i, p, g: (0, 0, 0), pipeline_mode=pl.Buffered(1))],
            out_specs=tuple(pl.BlockSpec((toks, w), lambda i, p, g: (0, 0)) for w in widths),
            scratch_shapes=[pltpu.VMEM((toks * sub, LANES), jnp.float32)],
        ),
        out_shape=tuple(jax.ShapeDtypeStruct((toks, w), jnp.bfloat16) for w in widths),
    )(pos, gates, rows)


def expert_body(rows_hbm, gate0, up0, down0, gate1, up1, down1, out_hbm,
                rows_ref, x_ref, acc_ref, gate_ref, up_ref, down_ref, hid_ref, in_sem, w_sem, out_sem, *, step, tile, cols):
    count, sub, _ = rows_hbm.shape
    hidden, width = down0.shape
    chunks = count // step
    ins = [
        pltpu.make_async_copy(rows_hbm.at[pl.ds(i * step, step)], rows_ref.at[pl.ds(i * step, step)], in_sem.at[i])
        for i in range(chunks)
    ]
    gates = [pltpu.make_async_copy(w, gate_ref.at[h], w_sem.at[h, 0]) for h, w in enumerate((gate0, gate1))]
    ups = [pltpu.make_async_copy(w, up_ref.at[h], w_sem.at[h, 1]) for h, w in enumerate((up0, up1))]
    downs = [pltpu.make_async_copy(w, down_ref.at[h], w_sem.at[h, 2]) for h, w in enumerate((down0, down1))]
    for c in ins[:2]:
        c.start()
    gates[0].start()
    for c in ins[2:]:
        c.start()
    for c in (ups[0], gates[1], ups[1], downs[0], downs[1]):
        c.start()
    for i in range(chunks):
        ins[i].wait()
        acc_ref[pl.ds(0, step * sub), :] = rows_ref[pl.ds(i * step, step)].astype(jnp.float32).reshape(step * sub, LANES)
        for j in range(sub):
            x_ref[pl.ds(i * step, step), j * LANES : (j + 1) * LANES] = acc_ref[
                pl.ds(j, step, stride=sub), :
            ].astype(jnp.bfloat16)
    contract = (((1,), (1,)), ((), ()))
    for h in range(2):
        gates[h].wait()
        ups[h].wait()
        for lo in range(0, hidden, tile):
            n = min(tile, hidden - lo)
            gate_val = lax.dot_general(x_ref[...], gate_ref[h, pl.ds(lo, n), :], contract, preferred_element_type=jnp.float32)
            up_val = lax.dot_general(x_ref[...], up_ref[h, pl.ds(lo, n), :], contract, preferred_element_type=jnp.float32)
            hid_ref[h, :, lo : lo + n] = (0.5 * gate_val * (1.0 + jnp.tanh(0.5 * gate_val)) * up_val).astype(jnp.bfloat16)
    for c in downs:
        c.wait()

    def down_step(d, carry):
        at = pl.ds(pl.multiple_of(d * cols, cols), cols)
        first = jnp.dot(hid_ref[0], down_ref[0, :, at], preferred_element_type=jnp.float32).astype(jnp.bfloat16)
        second = jnp.dot(hid_ref[1], down_ref[1, :, at], preferred_element_type=jnp.float32).astype(jnp.bfloat16)
        both = first.astype(jnp.float32) + second.astype(jnp.float32)
        for j in range(cols // LANES):
            acc_ref[pl.ds(d * (cols // LANES) + j, count, stride=sub), :] = both[:, j * LANES : (j + 1) * LANES]
        return carry

    lax.fori_loop(0, width // cols, down_step, 0)
    outs = [
        pltpu.make_async_copy(rows_ref.at[pl.ds(i * step, step)], out_hbm.at[pl.ds(i * step, step)], out_sem.at[i])
        for i in range(chunks)
    ]
    for i in range(chunks):
        rows_ref[pl.ds(i * step, step)] = (
            acc_ref[pl.ds(i * step * sub, step * sub), :].reshape(step, sub, LANES).astype(jnp.bfloat16)
        )
        outs[i].start()
    for c in outs:
        c.wait()


def expert(rows, gate0, up0, down0, gate1, up1, down1, step=128, tile=256, cols=256):
    count, sub, _ = rows.shape
    hidden, width = down0.shape
    chunks = count // step
    anywhere = pl.BlockSpec(memory_space=pl.ANY)
    return pl.pallas_call(
        functools.partial(expert_body, step=step, tile=tile, cols=cols),
        name="expert",
        in_specs=[anywhere] * 7,
        out_specs=anywhere,
        out_shape=jax.ShapeDtypeStruct(rows.shape, jnp.bfloat16),
        scratch_shapes=[
            pltpu.VMEM(rows.shape, jnp.bfloat16),
            pltpu.VMEM((count, width), jnp.bfloat16),
            pltpu.VMEM((count * sub, LANES), jnp.float32),
            pltpu.VMEM((2, hidden, width), jnp.bfloat16),
            pltpu.VMEM((2, hidden, width), jnp.bfloat16),
            pltpu.VMEM((2, hidden, width), jnp.bfloat16),
            pltpu.VMEM((2, count, hidden), jnp.bfloat16),
            pltpu.SemaphoreType.DMA((chunks,)),
            pltpu.SemaphoreType.DMA((2, 3)),
            pltpu.SemaphoreType.DMA((chunks,)),
        ],
        compiler_params=pltpu.CompilerParams(vmem_limit_bytes=60 * 1024 * 1024),
    )(rows, gate0, up0, down0, gate1, up1, down1)


VMEM_LIMIT = 60 * 1024 * 1024


def terms_body(at_ref, *refs, pieces, blocks, scale, apart):
    parts = refs[:pieces]
    cot_hbm, *out_hbm, all_rows, rows_ref, cot_ref, cut_ref, sem, side_sem, out_sem = refs[pieces:]
    loads = []
    for i, (piece, start, size) in enumerate(blocks):
        to = pl.ds(pl.multiple_of(at_ref[i], size), size)
        loads.append(pltpu.make_async_copy(parts[piece].at[pl.ds(start, size)], rows_ref.at[to], sem.at[i]))
    cot_load = pltpu.make_async_copy(cot_hbm, cot_ref, side_sem.at[0])
    cot_load.start()
    for c in loads:
        c.start()
    for c in loads:
        c.wait()
    keep = pltpu.make_async_copy(rows_ref, all_rows, side_sem.at[1])
    keep.start()
    cot_load.wait()
    owners = cut_ref.shape[0]

    def step(d, carry):
        at = pl.ds(pl.multiple_of(d * 2 * LANES, 2 * LANES), 2 * LANES)
        terms = jnp.dot(cot_ref[...], rows_ref[:, at], preferred_element_type=jnp.float32) * scale
        cut_ref[2 * d] = terms[:, :LANES].astype(jnp.bfloat16)
        cut_ref[2 * d + 1] = terms[:, LANES:].astype(jnp.bfloat16)
        return carry

    lax.fori_loop(0, owners // 2, step, 0)
    if apart:
        outs = [
            pltpu.make_async_copy(cut_ref.at[at_ref[len(blocks) + i]], out, out_sem.at[i]) for i, out in enumerate(out_hbm)
        ]
    else:
        outs = [pltpu.make_async_copy(cut_ref, out_hbm[0], out_sem.at[0])]
    for c in outs:
        c.start()
    for c in outs:
        c.wait()
    keep.wait()


def features_body(rows0, rows1, one_hbm, two_hbm, feat_one, feat_two, rows_ref, one_ref, two_ref, out_one, out_two, sem, row_sem, out_sem):
    count = rows0.shape[0]
    step = 512
    loads = []
    for half in range(2):
        loads.append(pltpu.make_async_copy(one_hbm.at[:, half], one_ref.at[half], sem.at[half, 0]))
        loads.append(pltpu.make_async_copy(two_hbm.at[:, half], two_ref.at[half], sem.at[half, 1]))
    for c in loads:
        c.start()

    def row_loads(i):
        at = pl.ds(i * step if isinstance(i, int) else pl.multiple_of(i * step, step), step)
        return [
            pltpu.make_async_copy(rows.at[at], rows_ref.at[half, at], row_sem.at[half, i])
            for half, rows in enumerate((rows0, rows1))
        ]

    def stores(i):
        at = pl.ds(i * step if isinstance(i, int) else pl.multiple_of(i * step, step), step)
        return [
            pltpu.make_async_copy(out_one.at[at], feat_one.at[at], out_sem.at[0, i]),
            pltpu.make_async_copy(out_two.at[at], feat_two.at[at], out_sem.at[1, i]),
        ]

    for i in range(count // step):
        for c in row_loads(i):
            c.start()
    for c in loads:
        c.wait()

    def body(i, carry):
        for c in row_loads(i):
            c.wait()
        at = pl.ds(pl.multiple_of(i * step, step), step)
        for w_ref, out_ref in ((one_ref, out_one), (two_ref, out_two)):
            for lo in range(0, w_ref.shape[-1], 256):
                total = [
                    jnp.dot(
                        rows_ref[half, at, :],
                        w_ref[half, :, :, lo : lo + 256].reshape(-1, 256),
                        preferred_element_type=jnp.float32,
                    )
                    for half in range(2)
                ]
                out_ref[at, lo : lo + 256] = (total[0] + total[1]).astype(jnp.bfloat16)
        for c in stores(i):
            c.start()
        return carry

    lax.fori_loop(0, count // step, body, 0)
    for i in range(count // step):
        for c in stores(i):
            c.wait()


def total_of(pieces):
    total = pieces[0].astype(jnp.float32)
    for piece in pieces[1:]:
        total = total + piece.astype(jnp.float32)
    return total.T


def sum_first_body(pieces_ref, out_ref):
    out_ref[...] = total_of([pieces_ref[i] for i in range(pieces_ref.shape[0])])


def sum_last_body(first_ref, *refs):
    *pieces, one_ref, two_ref = refs
    split = one_ref.shape[1]
    half = first_ref.shape[0]
    one_ref[:half] = first_ref[:, :split]
    two_ref[:half] = first_ref[:, split:]
    total = total_of([piece[...] for piece in pieces])
    one_ref[half:] = total[:, :split]
    two_ref[half:] = total[:, split:]


def project(parts, student_one, student_two, cots, move, pass_on, place):
    rows, half_width = parts[0].shape
    z, y_lo, y_hi, x, core = place
    ring, owners = 4, 8
    count = 4 * ring * rows
    split = student_one.shape[1]
    cols = split + student_two.shape[1]
    bf16, f32 = jnp.bfloat16, jnp.float32
    dma = pltpu.SemaphoreType.DMA
    anywhere = pl.BlockSpec(memory_space=pl.ANY)
    inside = pl.BlockSpec(memory_space=pltpu.VMEM)

    def row_of(y, at, c):
        return (y * ring + at % ring) * (2 * rows) + c * rows

    def spread(y, c):
        half = rows // 2
        near = [(0, rows, row_of(y, x + d, c)) for d in (0, ring - 1, 1)]
        return near + [(0, half, row_of(y, x + 2, c) + k * half) for k in range(2)]

    def gather(block):
        half = block.shape[0] // 2
        right = move(block, 0, 1, 0)
        left = move(block, 0, -1, 0)
        far_right = move(right[:half], 0, 1, 0)
        far_left = move(left[half:], 0, -1, 0)
        own = [block, right, left, far_right, far_left]
        swapped = []
        for piece in own:
            swapped.append(move(piece, 0, 0, 1))
        return own + swapped

    def single(y, first):
        return [(first + i, *spot) for i, spot in enumerate(spread(y, core) + spread(y, 1 - core))]

    def double(first):
        out = []
        for k, c in enumerate((core, 1 - core)):
            at = first + 5 * k
            for side, y in enumerate((y_hi, 1 - y_hi)):
                out += [(at + i, side * rows, rows, row_of(y, x + d, c)) for i, d in enumerate((0, ring - 1, 1))]
                out.append((at + 3 + side, 0, rows, row_of(y, x + 2, c)))
        return out

    steps = [(0, 0), (2, 1), (2, 0), (1, 1), (3, 1), (1, 0), (3, 0), (0, 1)]
    owner_of = [(z + dz) % 4 * 2 + (y_lo + dy) % 2 for dz, dy in steps]

    def terms(pieces, spots, apart):
        cuts = (owners * [jax.ShapeDtypeStruct((cols, LANES), bf16)]) if apart else [
            jax.ShapeDtypeStruct((owners, cols, LANES), bf16)
        ]
        blocks = tuple(spot[:3] for spot in spots)
        return pl.pallas_call(
            functools.partial(
                terms_body,
                pieces=len(pieces),
                blocks=blocks,
                scale=1.0 / math.sqrt(count * owners),
                apart=apart,
            ),
            name="terms",
            grid_spec=pltpu.PrefetchScalarGridSpec(
                num_scalar_prefetch=1,
                grid=(1,),
                in_specs=[anywhere] * (len(pieces) + 1),
                out_specs=(anywhere,) * (len(cuts) + 1),
                scratch_shapes=[
                    pltpu.VMEM((count, half_width), bf16),
                    pltpu.VMEM((cols, count), bf16),
                    pltpu.VMEM((owners, cols, LANES), bf16),
                    dma((len(blocks),)),
                    dma((2,)),
                    dma((owners,)),
                ],
            ),
            out_shape=(*cuts, jax.ShapeDtypeStruct((count, half_width), bf16)),
            compiler_params=pltpu.CompilerParams(vmem_limit_bytes=VMEM_LIMIT),
            cost_estimate=pl.CostEstimate(
                flops=2 * count * half_width * cols, transcendentals=0, bytes_accessed=12 << 20
            ),
        )(jnp.stack([spot[3] for spot in spots] + owner_of).astype(jnp.int32), *pieces, cots)

    other0 = move(parts[0], 2, 0, 0)
    other1 = move(parts[1], 2, 0, 0)
    cut0, rows0 = terms(gather(parts[0]) + gather(other0), single(y_hi, 0) + single(1 - y_hi, 10), False)
    cut0 = lax.all_to_all(cut0, "dp", split_axis=0, concat_axis=0, tiled=True)
    *cut1, rows1 = terms(gather(jnp.concatenate([parts[1], other1], axis=0)), double(0), True)
    for i, (dz, dy) in enumerate(steps[1:], 1):
        cut1[i] = pass_on(cut1[i], dz, dy)
    shape = (owners, 2, LANES)
    feat_one, feat_two = pl.pallas_call(
        features_body,
        name="features",
        in_specs=[anywhere] * 4,
        out_specs=(anywhere, anywhere),
        out_shape=(
            jax.ShapeDtypeStruct((count, split), bf16),
            jax.ShapeDtypeStruct((count, cols - split), bf16),
        ),
        scratch_shapes=[
            pltpu.VMEM((2, count, half_width), bf16),
            pltpu.VMEM((2, owners, LANES, split), bf16),
            pltpu.VMEM((2, owners, LANES, cols - split), bf16),
            pltpu.VMEM((count, split), bf16),
            pltpu.VMEM((count, cols - split), bf16),
            dma((2, 2)),
            dma((2, count // 512)),
            dma((2, count // 512)),
        ],
        compiler_params=pltpu.CompilerParams(vmem_limit_bytes=VMEM_LIMIT),
        cost_estimate=pl.CostEstimate(flops=4 * count * half_width * cols, transcendentals=0, bytes_accessed=14 << 20),
    )(rows0, rows1, student_one.reshape(*shape, split), student_two.reshape(*shape, cols - split))
    total0 = pl.pallas_call(
        sum_first_body,
        name="sum_first",
        in_specs=[inside],
        out_specs=inside,
        out_shape=jax.ShapeDtypeStruct((LANES, cols), f32),
    )(cut0)
    grad_one, grad_two = pl.pallas_call(
        sum_last_body,
        name="sum_last",
        in_specs=[inside] * (1 + owners),
        out_specs=(inside, inside),
        out_shape=(
            jax.ShapeDtypeStruct((2 * LANES, split), f32),
            jax.ShapeDtypeStruct((2 * LANES, cols - split), f32),
        ),
    )(total0, *cut1)
    return feat_one, feat_two, grad_one, grad_two


def local(
    tokens,
    norm_gain,
    expert_ids,
    gate_weights,
    gate_proj,
    up_proj,
    down_proj,
    student_one,
    student_two,
    cot_one,
    cot_two,
):
    tok_dev, model_width = tokens.shape
    top_count = expert_ids.shape[1]
    devices = lax.axis_size("dp") * lax.axis_size("expert")
    experts = devices // 2
    capacity = 2 * ((tok_dev * top_count * 7 + 12 * experts - 1) // (12 * experts))
    sub = model_width // LANES
    axes = ("dp", "expert")
    index = lax.axis_index(axes)

    def move(array, y, x, core):
        def target(d):
            z, y_lo, y_hi, at_x, at_core = d // 32, d // 16 % 2, d // 8 % 2, d // 2 % 4, d % 2
            to_y = (y_hi * 2 + y_lo + y) % 4
            return z * 32 + to_y % 2 * 16 + to_y // 2 * 8 + (at_x + x) % 4 * 2 + (at_core + core) % 2

        return lax.ppermute(array, axes, [(d, target(d)) for d in range(devices)])

    def pass_on(array, z, y_lo):
        def target(d):
            return (d // 32 + z) % 4 * 32 + (d // 16 + y_lo) % 2 * 16 + d % 16

        return lax.ppermute(array, axes, [(d, target(d)) for d in range(devices)])

    cots = jnp.concatenate([cot_one, cot_two], axis=1).T
    other_gate = move(jnp.swapaxes(gate_proj[0], 0, 1), 0, 0, 1)
    other_up = move(jnp.swapaxes(up_proj[0], 0, 1), 0, 0, 1)
    other_down, cots = lax.optimization_barrier((move(down_proj[0], 0, 0, 1), cots))

    placed, positions = dispatch(expert_ids.T, tokens, norm_gain.reshape(1, -1), experts, capacity)
    received = lax.all_to_all(
        placed.reshape(devices, capacity // 2, sub, LANES),
        ("dp", "expert"),
        split_axis=0,
        concat_axis=0,
        tiled=True,
    )
    expert_out = expert(
        received.reshape(devices * capacity // 2, sub, LANES),
        jnp.swapaxes(gate_proj[0], 0, 1),
        jnp.swapaxes(up_proj[0], 0, 1),
        down_proj[0],
        other_gate,
        other_up,
        other_down,
    )
    returned = lax.all_to_all(
        expert_out.reshape(devices, capacity // 2, sub, LANES),
        ("dp", "expert"),
        split_axis=0,
        concat_axis=0,
        tiled=True,
    )
    layer_out, *parts = combine(positions, gate_weights.T, returned.reshape(experts * capacity, sub, LANES))
    feat_one, feat_two, grad_one, grad_two = project(
        parts,
        student_one,
        student_two,
        cots,
        move,
        pass_on,
        (index // 32, index // 16 % 2, index // 8 % 2, index // 2 % 4, index % 2),
    )
    return (layer_out, feat_one, feat_two, grad_one, grad_two)


def solution(mesh):
    return jax.shard_map(
        local,
        mesh=mesh,
        in_specs=(
            P(("dp", "expert"), None),
            P(),
            P(("dp", "expert"), None),
            P(("dp", "expert"), None),
            P(("dp", "expert"), None, None),
            P(("dp", "expert"), None, None),
            P(("dp", "expert"), None, None),
            P(None, "expert"),
            P(None, "expert"),
            P("dp", "expert"),
            P("dp", "expert"),
        ),
        out_specs=(
            P(("dp", "expert"), None),
            P("dp", "expert"),
            P("dp", "expert"),
            P("dp", "expert"),
            P("dp", "expert"),
        ),
        check_vma=False,
    )
```

```python
import functools
import math

import jax
import jax.numpy as jnp
from jax import lax
from jax.experimental import pallas as pl
from jax.experimental.pallas import tpu as pltpu
from jax.sharding import PartitionSpec as P


LANES = 128


def dispatch_body(ids_ref, tok_ref, gain_ref, out_ref, pos_ref, rows_ref, pos_smem, sem, *, experts, cap):
    top, toks = ids_ref.shape
    width = tok_ref.shape[1]
    sub = width // LANES
    expert_iota = lax.broadcasted_iota(jnp.int32, (experts, toks), 0)
    named = [(ids_ref[k : k + 1, :] == expert_iota).astype(jnp.float32) for k in range(top)]
    total = named[0]
    for k in range(1, top):
        total = total + named[k]
    row = lax.broadcasted_iota(jnp.int32, (toks, toks), 0)
    col = lax.broadcasted_iota(jnp.int32, (toks, toks), 1)
    before = (row < col).astype(jnp.bfloat16)
    earlier = jnp.dot(total.astype(jnp.bfloat16), before, preferred_element_type=jnp.float32)
    for k in range(top):
        slot = jnp.sum(earlier * named[k], axis=0, keepdims=True)
        pos_ref[k : k + 1, :] = ids_ref[k : k + 1, :] * cap + slot.astype(jnp.int32)
    copy = pltpu.make_async_copy(pos_ref, pos_smem, sem)
    copy.start()
    out_ref[...] = jnp.zeros_like(out_ref)
    wide = tok_ref[...].astype(jnp.float32)
    mean_sq = jnp.mean(wide * wide, axis=-1, keepdims=True)
    normed = wide * lax.rsqrt(mean_sq + 1e-06) * gain_ref[...]
    for j in range(sub):
        rows_ref[pl.ds(j, toks, stride=sub), :] = normed[:, j * LANES : (j + 1) * LANES]
    copy.wait()

    def place(t, carry):
        one = rows_ref[pl.ds(pl.multiple_of(t * sub, sub), sub), :].astype(jnp.bfloat16)
        for k in range(top):
            out_ref[pos_smem[k, t]] = one
        return carry

    lax.fori_loop(0, toks, place, 0, unroll=4)


def dispatch(ids, tokens, gain, experts, cap):
    top, toks = ids.shape
    width = tokens.shape[1]
    sub = width // LANES
    return pl.pallas_call(
        functools.partial(dispatch_body, experts=experts, cap=cap),
        name="dispatch",
        out_shape=(
            jax.ShapeDtypeStruct((experts * cap, sub, LANES), jnp.bfloat16),
            jax.ShapeDtypeStruct((top, toks), jnp.int32),
        ),
        scratch_shapes=[
            pltpu.VMEM((toks * sub, LANES), jnp.float32),
            pltpu.SMEM((top, toks), jnp.int32),
            pltpu.SemaphoreType.DMA,
        ],
    )(ids, tokens, gain)


def combine_body(pos_ref, gates_ref, rows_ref, out_ref, even_ref, odd_ref, acc_ref):
    top, toks = pos_ref.shape
    sub = rows_ref.shape[1]

    def gather(t, carry):
        acc = rows_ref[pos_ref[0, t]].astype(jnp.float32) * gates_ref[0, t]
        for k in range(1, top):
            acc = acc + rows_ref[pos_ref[k, t]].astype(jnp.float32) * gates_ref[k, t]
        acc_ref[pl.ds(pl.multiple_of(t * sub, sub), sub), :] = acc
        return carry

    lax.fori_loop(0, toks, gather, 0, unroll=4)
    for j in range(sub):
        block = acc_ref[pl.ds(j, toks, stride=sub), :].astype(jnp.bfloat16)
        out_ref[:, j * LANES : (j + 1) * LANES] = block
        part_ref = (even_ref, odd_ref)[j % 2]
        part_ref[:, j // 2 * LANES : (j // 2 + 1) * LANES] = block


def combine(pos, gates, rows):
    _, toks = pos.shape
    sub = rows.shape[1]
    widths = (sub * LANES, sub // 2 * LANES, sub // 2 * LANES)
    return pl.pallas_call(
        combine_body,
        name="combine",
        grid_spec=pltpu.PrefetchScalarGridSpec(
            num_scalar_prefetch=2,
            grid=(1,),
            in_specs=[pl.BlockSpec(rows.shape, lambda i, p, g: (0, 0, 0), pipeline_mode=pl.Buffered(1))],
            out_specs=tuple(pl.BlockSpec((toks, w), lambda i, p, g: (0, 0)) for w in widths),
            scratch_shapes=[pltpu.VMEM((toks * sub, LANES), jnp.float32)],
        ),
        out_shape=tuple(jax.ShapeDtypeStruct((toks, w), jnp.bfloat16) for w in widths),
    )(pos, gates, rows)


def expert_body(rows_hbm, gate0, up0, down0, gate1, up1, down1, out_hbm,
                rows_ref, x_ref, acc_ref, gate_ref, up_ref, down_ref, hid_ref, in_sem, w_sem, out_sem, *, step, tile, cols):
    count, sub, _ = rows_hbm.shape
    hidden, width = down0.shape
    chunks = count // step
    ins = [
        pltpu.make_async_copy(rows_hbm.at[pl.ds(i * step, step)], rows_ref.at[pl.ds(i * step, step)], in_sem.at[i])
        for i in range(chunks)
    ]
    gates = [pltpu.make_async_copy(w, gate_ref.at[h], w_sem.at[h, 0]) for h, w in enumerate((gate0, gate1))]
    ups = [pltpu.make_async_copy(w, up_ref.at[h], w_sem.at[h, 1]) for h, w in enumerate((up0, up1))]
    downs = [pltpu.make_async_copy(w, down_ref.at[h], w_sem.at[h, 2]) for h, w in enumerate((down0, down1))]
    for c in ins[:2]:
        c.start()
    gates[0].start()
    for c in ins[2:]:
        c.start()
    for c in (ups[0], gates[1], ups[1], downs[0], downs[1]):
        c.start()
    for i in range(chunks):
        ins[i].wait()
        acc_ref[pl.ds(0, step * sub), :] = rows_ref[pl.ds(i * step, step)].astype(jnp.float32).reshape(step * sub, LANES)
        for j in range(sub):
            x_ref[pl.ds(i * step, step), j * LANES : (j + 1) * LANES] = acc_ref[
                pl.ds(j, step, stride=sub), :
            ].astype(jnp.bfloat16)
    contract = (((1,), (1,)), ((), ()))
    for h in range(2):
        gates[h].wait()
        ups[h].wait()
        for lo in range(0, hidden, tile):
            n = min(tile, hidden - lo)
            gate_val = lax.dot_general(x_ref[...], gate_ref[h, pl.ds(lo, n), :], contract, preferred_element_type=jnp.float32)
            up_val = lax.dot_general(x_ref[...], up_ref[h, pl.ds(lo, n), :], contract, preferred_element_type=jnp.float32)
            hid_ref[h, :, lo : lo + n] = (0.5 * gate_val * (1.0 + jnp.tanh(0.5 * gate_val)) * up_val).astype(jnp.bfloat16)
    for c in downs:
        c.wait()

    def down_step(d, carry):
        at = pl.ds(pl.multiple_of(d * cols, cols), cols)
        first = jnp.dot(hid_ref[0], down_ref[0, :, at], preferred_element_type=jnp.float32).astype(jnp.bfloat16)
        second = jnp.dot(hid_ref[1], down_ref[1, :, at], preferred_element_type=jnp.float32).astype(jnp.bfloat16)
        both = first.astype(jnp.float32) + second.astype(jnp.float32)
        for j in range(cols // LANES):
            acc_ref[pl.ds(d * (cols // LANES) + j, count, stride=sub), :] = both[:, j * LANES : (j + 1) * LANES]
        return carry

    lax.fori_loop(0, width // cols, down_step, 0)
    outs = [
        pltpu.make_async_copy(rows_ref.at[pl.ds(i * step, step)], out_hbm.at[pl.ds(i * step, step)], out_sem.at[i])
        for i in range(chunks)
    ]
    for i in range(chunks):
        rows_ref[pl.ds(i * step, step)] = (
            acc_ref[pl.ds(i * step * sub, step * sub), :].reshape(step, sub, LANES).astype(jnp.bfloat16)
        )
        outs[i].start()
    for c in outs:
        c.wait()


def expert(rows, gate0, up0, down0, gate1, up1, down1, step=128, tile=256, cols=256):
    count, sub, _ = rows.shape
    hidden, width = down0.shape
    chunks = count // step
    anywhere = pl.BlockSpec(memory_space=pl.ANY)
    return pl.pallas_call(
        functools.partial(expert_body, step=step, tile=tile, cols=cols),
        name="expert",
        in_specs=[anywhere] * 7,
        out_specs=anywhere,
        out_shape=jax.ShapeDtypeStruct(rows.shape, jnp.bfloat16),
        scratch_shapes=[
            pltpu.VMEM(rows.shape, jnp.bfloat16),
            pltpu.VMEM((count, width), jnp.bfloat16),
            pltpu.VMEM((count * sub, LANES), jnp.float32),
            pltpu.VMEM((2, hidden, width), jnp.bfloat16),
            pltpu.VMEM((2, hidden, width), jnp.bfloat16),
            pltpu.VMEM((2, hidden, width), jnp.bfloat16),
            pltpu.VMEM((2, count, hidden), jnp.bfloat16),
            pltpu.SemaphoreType.DMA((chunks,)),
            pltpu.SemaphoreType.DMA((2, 3)),
            pltpu.SemaphoreType.DMA((chunks,)),
        ],
        compiler_params=pltpu.CompilerParams(vmem_limit_bytes=60 * 1024 * 1024),
    )(rows, gate0, up0, down0, gate1, up1, down1)


VMEM_LIMIT = 60 * 1024 * 1024


def terms_body(at_ref, *refs, pieces, blocks, scale):
    parts = refs[:pieces]
    cot_hbm, out_hbm, all_rows, rows_ref, cot_ref, cut_ref, sem, side_sem, out_sem = refs[pieces:]
    loads = []
    for i, (piece, start, size) in enumerate(blocks):
        to = pl.ds(pl.multiple_of(at_ref[i], size), size)
        loads.append(pltpu.make_async_copy(parts[piece].at[pl.ds(start, size)], rows_ref.at[to], sem.at[i]))
    cot_load = pltpu.make_async_copy(cot_hbm, cot_ref, side_sem.at[0])
    cot_load.start()
    for c in loads:
        c.start()
    for c in loads:
        c.wait()
    keep = pltpu.make_async_copy(rows_ref, all_rows, side_sem.at[1])
    keep.start()
    cot_load.wait()
    owners = cut_ref.shape[0]

    def step(d, carry):
        at = pl.ds(pl.multiple_of(d * 2 * LANES, 2 * LANES), 2 * LANES)
        terms = jnp.dot(cot_ref[...], rows_ref[:, at], preferred_element_type=jnp.float32) * scale
        cut_ref[2 * d] = terms[:, :LANES].astype(jnp.bfloat16)
        cut_ref[2 * d + 1] = terms[:, LANES:].astype(jnp.bfloat16)
        return carry

    lax.fori_loop(0, owners // 2, step, 0)
    out = pltpu.make_async_copy(cut_ref, out_hbm, out_sem)
    out.start()
    out.wait()
    keep.wait()


def part_body(at_ref, *refs, pieces, blocks, scale, last):
    parts = refs[:pieces]
    if last:
        cot_hbm, near_hbm, _, *out_hbm, all_rows = refs[pieces : pieces + 12]
    else:
        cot_hbm, near_hbm, all_rows = refs[pieces : pieces + 3]
    rows_ref, cot_ref, acc_ref, cut_ref, sem, cot_sem, keep_sem, acc_sem, out_sem = refs[-9:]
    size = LANES
    loads, cot_loads, keeps = [], [], []
    for i, (piece, start, _) in enumerate(blocks):
        to = pl.ds(pl.multiple_of(at_ref[i], size), size)
        here = pl.ds(i * size, size)
        loads.append(pltpu.make_async_copy(parts[piece].at[pl.ds(start, size)], rows_ref.at[here], sem.at[i]))
        cot_loads.append(pltpu.make_async_copy(cot_hbm.at[:, to], cot_ref.at[:, here], cot_sem.at[i]))
        keeps.append(pltpu.make_async_copy(rows_ref.at[here], all_rows.at[to], keep_sem.at[i]))
    owners = cut_ref.shape[0]
    wide = 2 * LANES
    for c in loads + cot_loads:
        c.start()

    def sums(d):
        at = pl.ds(d * wide if isinstance(d, int) else pl.multiple_of(d * wide, wide), wide)
        ends = (near_hbm.at[:, at], acc_ref.at[:, at]) if last else (acc_ref.at[:, at], near_hbm.at[:, at])
        return pltpu.make_async_copy(*ends, acc_sem.at[d])

    if last:
        for d in range(owners // 2):
            sums(d).start()
    for c in loads:
        c.wait()
    for c in keeps:
        c.start()
    for c in cot_loads:
        c.wait()

    def step(d, carry):
        at = pl.ds(pl.multiple_of(d * wide, wide), wide)
        terms = jnp.dot(cot_ref[...], rows_ref[:, at], preferred_element_type=jnp.float32)
        if last:
            sums(d).wait()
            terms = (terms + acc_ref[:, at]) * scale
            cut_ref[2 * d] = terms[:, :LANES].astype(jnp.bfloat16)
            cut_ref[2 * d + 1] = terms[:, LANES:].astype(jnp.bfloat16)
        else:
            acc_ref[:, at] = terms
            sums(d).start()
        return carry

    lax.fori_loop(0, owners // 2, step, 0)
    if last:
        outs = [
            pltpu.make_async_copy(cut_ref.at[at_ref[len(blocks) + i]], out, out_sem.at[i]) for i, out in enumerate(out_hbm)
        ]
        for c in outs:
            c.start()
        for c in outs:
            c.wait()
    else:
        for d in range(owners // 2):
            sums(d).wait()
    for c in keeps:
        c.wait()


def features_body(rows0, rows1, one_hbm, two_hbm, feat_one, feat_two, rows_ref, one_ref, two_ref, out_one, out_two, sem, row_sem, out_sem):
    count = rows0.shape[0]
    step = 512
    loads = []
    for half in range(2):
        loads.append(pltpu.make_async_copy(one_hbm.at[:, half], one_ref.at[half], sem.at[half, 0]))
        loads.append(pltpu.make_async_copy(two_hbm.at[:, half], two_ref.at[half], sem.at[half, 1]))
    for c in loads:
        c.start()

    def row_loads(i):
        at = pl.ds(i * step if isinstance(i, int) else pl.multiple_of(i * step, step), step)
        return [
            pltpu.make_async_copy(rows.at[at], rows_ref.at[half, at], row_sem.at[half, i])
            for half, rows in enumerate((rows0, rows1))
        ]

    def stores(i):
        at = pl.ds(i * step if isinstance(i, int) else pl.multiple_of(i * step, step), step)
        return [
            pltpu.make_async_copy(out_one.at[at], feat_one.at[at], out_sem.at[0, i]),
            pltpu.make_async_copy(out_two.at[at], feat_two.at[at], out_sem.at[1, i]),
        ]

    for i in range(count // step):
        for c in row_loads(i):
            c.start()
    for c in loads:
        c.wait()

    def body(i, carry):
        for c in row_loads(i):
            c.wait()
        at = pl.ds(pl.multiple_of(i * step, step), step)
        for w_ref, out_ref in ((one_ref, out_one), (two_ref, out_two)):
            for lo in range(0, w_ref.shape[-1], 256):
                total = [
                    jnp.dot(
                        rows_ref[half, at, :],
                        w_ref[half, :, :, lo : lo + 256].reshape(-1, 256),
                        preferred_element_type=jnp.float32,
                    )
                    for half in range(2)
                ]
                out_ref[at, lo : lo + 256] = (total[0] + total[1]).astype(jnp.bfloat16)
        for c in stores(i):
            c.start()
        return carry

    lax.fori_loop(0, count // step, body, 0)
    for i in range(count // step):
        for c in stores(i):
            c.wait()


def total_of(pieces):
    total = pieces[0].astype(jnp.float32)
    for piece in pieces[1:]:
        total = total + piece.astype(jnp.float32)
    return total.T


def sum_first_body(pieces_ref, out_ref):
    out_ref[...] = total_of([pieces_ref[i] for i in range(pieces_ref.shape[0])])


def sum_last_body(first_ref, *refs):
    *pieces, one_ref, two_ref = refs
    split = one_ref.shape[1]
    half = first_ref.shape[0]
    one_ref[:half] = first_ref[:, :split]
    two_ref[:half] = first_ref[:, split:]
    total = total_of([piece[...] for piece in pieces])
    one_ref[half:] = total[:, :split]
    two_ref[half:] = total[:, split:]


def project(parts, student_one, student_two, cots, move, pass_on, place):
    rows, half_width = parts[0].shape
    z, y_lo, y_hi, x, core = place
    ring, owners = 4, 8
    count = 4 * ring * rows
    split = student_one.shape[1]
    cols = split + student_two.shape[1]
    bf16, f32 = jnp.bfloat16, jnp.float32
    dma = pltpu.SemaphoreType.DMA
    anywhere = pl.BlockSpec(memory_space=pl.ANY)
    inside = pl.BlockSpec(memory_space=pltpu.VMEM)

    def row_of(y, at, c):
        return (y * ring + at % ring) * (2 * rows) + c * rows

    def spread(y, c):
        half = rows // 2
        near = [(0, rows, row_of(y, x + d, c)) for d in (0, ring - 1, 1)]
        return near + [(0, half, row_of(y, x + 2, c) + k * half) for k in range(2)]

    def gather(block):
        half = block.shape[0] // 2
        right = move(block, 0, 1, 0)
        left = move(block, 0, -1, 0)
        far_right = move(right[:half], 0, 1, 0)
        far_left = move(left[half:], 0, -1, 0)
        own = [block, right, left, far_right, far_left]
        swapped = []
        for piece in own:
            swapped.append(move(piece, 0, 0, 1))
        return own + swapped

    def single(y, first):
        return [(first + i, *spot) for i, spot in enumerate(spread(y, core) + spread(y, 1 - core))]

    def double(first):
        out = []
        for k, c in enumerate((core, 1 - core)):
            at = first + 5 * k
            for side, y in enumerate((y_hi, 1 - y_hi)):
                out += [(at + i, side * rows, rows, row_of(y, x + d, c)) for i, d in enumerate((0, ring - 1, 1))]
                out.append((at + 3 + side, 0, rows, row_of(y, x + 2, c)))
        return out

    steps = [(0, 0), (2, 1), (2, 0), (1, 1), (3, 1), (1, 0), (3, 0), (0, 1)]
    owner_of = [(z + dz) % 4 * 2 + (y_lo + dy) % 2 for dz, dy in steps]

    scale = 1.0 / math.sqrt(count * owners)

    def call(body, pieces, spots, others, outs, scratch, aliases, flops):
        rows_of = jnp.stack([spot[3] for spot in spots] + owner_of).astype(jnp.int32)
        return pl.pallas_call(
            functools.partial(body, pieces=len(pieces), blocks=tuple(spot[:3] for spot in spots), scale=scale),
            grid_spec=pltpu.PrefetchScalarGridSpec(
                num_scalar_prefetch=1,
                grid=(1,),
                in_specs=[anywhere] * (len(pieces) + len(others)),
                out_specs=(anywhere,) * len(outs),
                scratch_shapes=scratch,
            ),
            out_shape=outs,
            input_output_aliases=aliases,
            compiler_params=pltpu.CompilerParams(vmem_limit_bytes=VMEM_LIMIT),
            cost_estimate=pl.CostEstimate(flops=flops, transcendentals=0, bytes_accessed=10 << 20),
        )(rows_of, *pieces, *others)

    rows_shape = jax.ShapeDtypeStruct((count, half_width), bf16)
    near_shape = jax.ShapeDtypeStruct((cols, half_width), f32)
    cut_vmem = pltpu.VMEM((owners, cols, LANES), bf16)

    def terms(pieces, spots):
        scratch = [pltpu.VMEM((count, half_width), bf16), pltpu.VMEM((cols, count), bf16), cut_vmem]
        return call(
            terms_body,
            pieces,
            spots,
            [cots],
            (jax.ShapeDtypeStruct((owners, cols, LANES), bf16), rows_shape),
            scratch + [dma((len(spots),)), dma((2,)), dma],
            {},
            2 * count * half_width * cols,
        )

    def part(pieces, spots, others, outs, aliases, last):
        number = len(spots)
        scratch = [
            pltpu.VMEM((number * LANES, half_width), bf16),
            pltpu.VMEM((cols, number * LANES), bf16),
            pltpu.VMEM((cols, half_width), f32),
            cut_vmem,
        ]
        scratch += [dma((number,)), dma((number,)), dma((number,)), dma((owners // 2,)), dma((owners,))]
        body = functools.partial(part_body, last=last)
        return call(body, pieces, spots, others, outs, scratch, aliases, 2 * number * LANES * half_width * cols)

    other0 = move(parts[0], 2, 0, 0)
    other1 = move(parts[1], 2, 0, 0)
    cut0, rows0 = terms(gather(parts[0]) + gather(other0), single(y_hi, 0) + single(1 - y_hi, 10))
    cut0 = lax.all_to_all(cut0, "dp", split_axis=0, concat_axis=0, tiled=True)
    pieces, spots = gather(jnp.concatenate([parts[1], other1], axis=0)), double(0)
    at_once = [spot for spot in spots if spot[0] % 5 < 3]
    later = [(spot[0] // 5 * 2 + spot[0] % 5 - 3, *spot[1:]) for spot in spots if spot[0] % 5 >= 3]
    near_pieces = pieces[0:3] + pieces[5:8]
    at_once = [(spot[0] // 5 * 3 + spot[0] % 5, *spot[1:]) for spot in at_once]
    near_terms, rows1 = part(near_pieces, at_once, [cots], (near_shape, rows_shape), {}, False)
    *cut1, rows1 = part(
        pieces[3:5] + pieces[8:10],
        later,
        [cots, near_terms, rows1],
        owners * (jax.ShapeDtypeStruct((cols, LANES), bf16),) + (rows_shape,),
        {7: owners},
        True,
    )
    for i, (dz, dy) in enumerate(steps[1:], 1):
        cut1[i] = pass_on(cut1[i], dz, dy)
    shape = (owners, 2, LANES)
    feat_one, feat_two = pl.pallas_call(
        features_body,
        name="features",
        in_specs=[anywhere] * 4,
        out_specs=(anywhere, anywhere),
        out_shape=(
            jax.ShapeDtypeStruct((count, split), bf16),
            jax.ShapeDtypeStruct((count, cols - split), bf16),
        ),
        scratch_shapes=[
            pltpu.VMEM((2, count, half_width), bf16),
            pltpu.VMEM((2, owners, LANES, split), bf16),
            pltpu.VMEM((2, owners, LANES, cols - split), bf16),
            pltpu.VMEM((count, split), bf16),
            pltpu.VMEM((count, cols - split), bf16),
            dma((2, 2)),
            dma((2, count // 512)),
            dma((2, count // 512)),
        ],
        compiler_params=pltpu.CompilerParams(vmem_limit_bytes=VMEM_LIMIT),
        cost_estimate=pl.CostEstimate(flops=4 * count * half_width * cols, transcendentals=0, bytes_accessed=14 << 20),
    )(rows0, rows1, student_one.reshape(*shape, split), student_two.reshape(*shape, cols - split))
    total0 = pl.pallas_call(
        sum_first_body,
        name="sum_first",
        in_specs=[inside],
        out_specs=inside,
        out_shape=jax.ShapeDtypeStruct((LANES, cols), f32),
    )(cut0)
    grad_one, grad_two = pl.pallas_call(
        sum_last_body,
        name="sum_last",
        in_specs=[inside] * (1 + owners),
        out_specs=(inside, inside),
        out_shape=(
            jax.ShapeDtypeStruct((2 * LANES, split), f32),
            jax.ShapeDtypeStruct((2 * LANES, cols - split), f32),
        ),
    )(total0, *cut1)
    return feat_one, feat_two, grad_one, grad_two


def local(
    tokens,
    norm_gain,
    expert_ids,
    gate_weights,
    gate_proj,
    up_proj,
    down_proj,
    student_one,
    student_two,
    cot_one,
    cot_two,
):
    tok_dev, model_width = tokens.shape
    top_count = expert_ids.shape[1]
    devices = lax.axis_size("dp") * lax.axis_size("expert")
    experts = devices // 2
    capacity = 2 * ((tok_dev * top_count * 7 + 12 * experts - 1) // (12 * experts))
    sub = model_width // LANES
    axes = ("dp", "expert")
    index = lax.axis_index(axes)

    def move(array, y, x, core):
        def target(d):
            z, y_lo, y_hi, at_x, at_core = d // 32, d // 16 % 2, d // 8 % 2, d // 2 % 4, d % 2
            to_y = (y_hi * 2 + y_lo + y) % 4
            return z * 32 + to_y % 2 * 16 + to_y // 2 * 8 + (at_x + x) % 4 * 2 + (at_core + core) % 2

        return lax.ppermute(array, axes, [(d, target(d)) for d in range(devices)])

    def pass_on(array, z, y_lo):
        def target(d):
            return (d // 32 + z) % 4 * 32 + (d // 16 + y_lo) % 2 * 16 + d % 16

        return lax.ppermute(array, axes, [(d, target(d)) for d in range(devices)])

    cots = jnp.concatenate([cot_one, cot_two], axis=1).T
    other_gate = move(jnp.swapaxes(gate_proj[0], 0, 1), 0, 0, 1)
    other_up = move(jnp.swapaxes(up_proj[0], 0, 1), 0, 0, 1)
    other_down, cots = lax.optimization_barrier((move(down_proj[0], 0, 0, 1), cots))

    placed, positions = dispatch(expert_ids.T, tokens, norm_gain.reshape(1, -1), experts, capacity)
    received = lax.all_to_all(
        placed.reshape(devices, capacity // 2, sub, LANES),
        ("dp", "expert"),
        split_axis=0,
        concat_axis=0,
        tiled=True,
    )
    expert_out = expert(
        received.reshape(devices * capacity // 2, sub, LANES),
        jnp.swapaxes(gate_proj[0], 0, 1),
        jnp.swapaxes(up_proj[0], 0, 1),
        down_proj[0],
        other_gate,
        other_up,
        other_down,
    )
    returned = lax.all_to_all(
        expert_out.reshape(devices, capacity // 2, sub, LANES),
        ("dp", "expert"),
        split_axis=0,
        concat_axis=0,
        tiled=True,
    )
    layer_out, *parts = combine(positions, gate_weights.T, returned.reshape(experts * capacity, sub, LANES))
    feat_one, feat_two, grad_one, grad_two = project(
        parts,
        student_one,
        student_two,
        cots,
        move,
        pass_on,
        (index // 32, index // 16 % 2, index // 8 % 2, index // 2 % 4, index % 2),
    )
    return (layer_out, feat_one, feat_two, grad_one, grad_two)


def solution(mesh):
    return jax.shard_map(
        local,
        mesh=mesh,
        in_specs=(
            P(("dp", "expert"), None),
            P(),
            P(("dp", "expert"), None),
            P(("dp", "expert"), None),
            P(("dp", "expert"), None, None),
            P(("dp", "expert"), None, None),
            P(("dp", "expert"), None, None),
            P(None, "expert"),
            P(None, "expert"),
            P("dp", "expert"),
            P("dp", "expert"),
        ),
        out_specs=(
            P(("dp", "expert"), None),
            P("dp", "expert"),
            P("dp", "expert"),
            P("dp", "expert"),
            P("dp", "expert"),
        ),
        check_vma=False,
    )
```

```python
import functools
import math

import jax
import jax.numpy as jnp
from jax import lax
from jax.experimental import pallas as pl
from jax.experimental.pallas import tpu as pltpu
from jax.sharding import PartitionSpec as P


LANES = 128


def dispatch_body(ids_ref, tok_ref, gain_ref, out_ref, pos_ref, rows_ref, pos_smem, sem, *, experts, cap):
    top, toks = ids_ref.shape
    width = tok_ref.shape[1]
    sub = width // LANES
    expert_iota = lax.broadcasted_iota(jnp.int32, (experts, toks), 0)
    named = [(ids_ref[k : k + 1, :] == expert_iota).astype(jnp.float32) for k in range(top)]
    total = named[0]
    for k in range(1, top):
        total = total + named[k]
    row = lax.broadcasted_iota(jnp.int32, (toks, toks), 0)
    col = lax.broadcasted_iota(jnp.int32, (toks, toks), 1)
    before = (row < col).astype(jnp.bfloat16)
    earlier = jnp.dot(total.astype(jnp.bfloat16), before, preferred_element_type=jnp.float32)
    for k in range(top):
        slot = jnp.sum(earlier * named[k], axis=0, keepdims=True)
        pos_ref[k : k + 1, :] = ids_ref[k : k + 1, :] * cap + slot.astype(jnp.int32)
    copy = pltpu.make_async_copy(pos_ref, pos_smem, sem)
    copy.start()
    out_ref[...] = jnp.zeros_like(out_ref)
    wide = tok_ref[...].astype(jnp.float32)
    mean_sq = jnp.mean(wide * wide, axis=-1, keepdims=True)
    normed = wide * lax.rsqrt(mean_sq + 1e-06) * gain_ref[...]
    for j in range(sub):
        rows_ref[pl.ds(j, toks, stride=sub), :] = normed[:, j * LANES : (j + 1) * LANES]
    copy.wait()

    def place(t, carry):
        one = rows_ref[pl.ds(pl.multiple_of(t * sub, sub), sub), :].astype(jnp.bfloat16)
        for k in range(top):
            out_ref[pos_smem[k, t]] = one
        return carry

    lax.fori_loop(0, toks, place, 0, unroll=4)


def dispatch(ids, tokens, gain, experts, cap):
    top, toks = ids.shape
    width = tokens.shape[1]
    sub = width // LANES
    return pl.pallas_call(
        functools.partial(dispatch_body, experts=experts, cap=cap),
        name="dispatch",
        out_shape=(
            jax.ShapeDtypeStruct((experts * cap, sub, LANES), jnp.bfloat16),
            jax.ShapeDtypeStruct((top, toks), jnp.int32),
        ),
        scratch_shapes=[
            pltpu.VMEM((toks * sub, LANES), jnp.float32),
            pltpu.SMEM((top, toks), jnp.int32),
            pltpu.SemaphoreType.DMA,
        ],
    )(ids, tokens, gain)


def combine_body(pos_ref, gates_ref, rows_ref, out_ref, even_ref, odd_ref, acc_ref):
    top, toks = pos_ref.shape
    sub = rows_ref.shape[1]

    def gather(t, carry):
        acc = rows_ref[pos_ref[0, t]].astype(jnp.float32) * gates_ref[0, t]
        for k in range(1, top):
            acc = acc + rows_ref[pos_ref[k, t]].astype(jnp.float32) * gates_ref[k, t]
        acc_ref[pl.ds(pl.multiple_of(t * sub, sub), sub), :] = acc
        return carry

    lax.fori_loop(0, toks, gather, 0, unroll=4)
    for j in range(sub):
        block = acc_ref[pl.ds(j, toks, stride=sub), :].astype(jnp.bfloat16)
        out_ref[:, j * LANES : (j + 1) * LANES] = block
        part_ref = (even_ref, odd_ref)[j % 2]
        part_ref[:, j // 2 * LANES : (j // 2 + 1) * LANES] = block


def combine(pos, gates, rows):
    _, toks = pos.shape
    sub = rows.shape[1]
    widths = (sub * LANES, sub // 2 * LANES, sub // 2 * LANES)
    return pl.pallas_call(
        combine_body,
        name="combine",
        grid_spec=pltpu.PrefetchScalarGridSpec(
            num_scalar_prefetch=2,
            grid=(1,),
            in_specs=[pl.BlockSpec(rows.shape, lambda i, p, g: (0, 0, 0), pipeline_mode=pl.Buffered(1))],
            out_specs=tuple(pl.BlockSpec((toks, w), lambda i, p, g: (0, 0)) for w in widths),
            scratch_shapes=[pltpu.VMEM((toks * sub, LANES), jnp.float32)],
        ),
        out_shape=tuple(jax.ShapeDtypeStruct((toks, w), jnp.bfloat16) for w in widths),
    )(pos, gates, rows)


def expert_body(rows_hbm, gate0, up0, down0, gate1, up1, down1, out_hbm,
                rows_ref, x_ref, acc_ref, gate_ref, up_ref, down_ref, hid_ref, in_sem, w_sem, out_sem, *, step, tile, cols):
    count, sub, _ = rows_hbm.shape
    hidden, width = down0.shape
    chunks = count // step
    ins = [
        pltpu.make_async_copy(rows_hbm.at[pl.ds(i * step, step)], rows_ref.at[pl.ds(i * step, step)], in_sem.at[i])
        for i in range(chunks)
    ]
    gates = [pltpu.make_async_copy(w, gate_ref.at[h], w_sem.at[h, 0]) for h, w in enumerate((gate0, gate1))]
    ups = [pltpu.make_async_copy(w, up_ref.at[h], w_sem.at[h, 1]) for h, w in enumerate((up0, up1))]
    downs = [pltpu.make_async_copy(w, down_ref.at[h], w_sem.at[h, 2]) for h, w in enumerate((down0, down1))]
    for c in ins[:2]:
        c.start()
    gates[0].start()
    for c in ins[2:]:
        c.start()
    for c in (ups[0], gates[1], ups[1], downs[0], downs[1]):
        c.start()
    for i in range(chunks):
        ins[i].wait()
        acc_ref[pl.ds(0, step * sub), :] = rows_ref[pl.ds(i * step, step)].astype(jnp.float32).reshape(step * sub, LANES)
        for j in range(sub):
            x_ref[pl.ds(i * step, step), j * LANES : (j + 1) * LANES] = acc_ref[
                pl.ds(j, step, stride=sub), :
            ].astype(jnp.bfloat16)
    contract = (((1,), (1,)), ((), ()))
    for h in range(2):
        gates[h].wait()
        ups[h].wait()
        for lo in range(0, hidden, tile):
            n = min(tile, hidden - lo)
            gate_val = lax.dot_general(x_ref[...], gate_ref[h, pl.ds(lo, n), :], contract, preferred_element_type=jnp.float32)
            up_val = lax.dot_general(x_ref[...], up_ref[h, pl.ds(lo, n), :], contract, preferred_element_type=jnp.float32)
            hid_ref[h, :, lo : lo + n] = (0.5 * gate_val * (1.0 + jnp.tanh(0.5 * gate_val)) * up_val).astype(jnp.bfloat16)
    for c in downs:
        c.wait()

    def down_step(d, carry):
        at = pl.ds(pl.multiple_of(d * cols, cols), cols)
        first = jnp.dot(hid_ref[0], down_ref[0, :, at], preferred_element_type=jnp.float32).astype(jnp.bfloat16)
        second = jnp.dot(hid_ref[1], down_ref[1, :, at], preferred_element_type=jnp.float32).astype(jnp.bfloat16)
        both = first.astype(jnp.float32) + second.astype(jnp.float32)
        for j in range(cols // LANES):
            acc_ref[pl.ds(d * (cols // LANES) + j, count, stride=sub), :] = both[:, j * LANES : (j + 1) * LANES]
        return carry

    lax.fori_loop(0, width // cols, down_step, 0)
    outs = [
        pltpu.make_async_copy(rows_ref.at[pl.ds(i * step, step)], out_hbm.at[pl.ds(i * step, step)], out_sem.at[i])
        for i in range(chunks)
    ]
    for i in range(chunks):
        rows_ref[pl.ds(i * step, step)] = (
            acc_ref[pl.ds(i * step * sub, step * sub), :].reshape(step, sub, LANES).astype(jnp.bfloat16)
        )
        outs[i].start()
    for c in outs:
        c.wait()


def expert(rows, gate0, up0, down0, gate1, up1, down1, step=128, tile=256, cols=256):
    count, sub, _ = rows.shape
    hidden, width = down0.shape
    chunks = count // step
    anywhere = pl.BlockSpec(memory_space=pl.ANY)
    return pl.pallas_call(
        functools.partial(expert_body, step=step, tile=tile, cols=cols),
        name="expert",
        in_specs=[anywhere] * 7,
        out_specs=anywhere,
        out_shape=jax.ShapeDtypeStruct(rows.shape, jnp.bfloat16),
        scratch_shapes=[
            pltpu.VMEM(rows.shape, jnp.bfloat16),
            pltpu.VMEM((count, width), jnp.bfloat16),
            pltpu.VMEM((count * sub, LANES), jnp.float32),
            pltpu.VMEM((2, hidden, width), jnp.bfloat16),
            pltpu.VMEM((2, hidden, width), jnp.bfloat16),
            pltpu.VMEM((2, hidden, width), jnp.bfloat16),
            pltpu.VMEM((2, count, hidden), jnp.bfloat16),
            pltpu.SemaphoreType.DMA((chunks,)),
            pltpu.SemaphoreType.DMA((2, 3)),
            pltpu.SemaphoreType.DMA((chunks,)),
        ],
        compiler_params=pltpu.CompilerParams(vmem_limit_bytes=60 * 1024 * 1024),
    )(rows, gate0, up0, down0, gate1, up1, down1)


VMEM_LIMIT = 60 * 1024 * 1024


def terms_body(at_ref, *refs, pieces, blocks, base, owners_at, scale, apart):
    parts = refs[:pieces]
    cot_hbm, *out_hbm, all_rows, rows_ref, cot_ref, cut_ref, sem, keep_sem, cot_sem, out_sem = refs[pieces:]
    owners = cut_ref.shape[0]
    wide = 2 * LANES
    tiles = owners // 2

    def columns(d):
        return pl.ds(d * wide if isinstance(d, int) else pl.multiple_of(d * wide, wide), wide)

    def loads(d):
        for i, (piece, start, size) in enumerate(blocks):
            to = pl.ds(pl.multiple_of(at_ref[base + i], size), size)
            ends = parts[piece].at[pl.ds(start, size), columns(d)], rows_ref.at[to, columns(d)]
            yield pltpu.make_async_copy(*ends, sem.at[d, i])

    def keep(d):
        return pltpu.make_async_copy(rows_ref.at[:, columns(d)], all_rows.at[:, columns(d)], keep_sem.at[d])

    cot_load = pltpu.make_async_copy(cot_hbm, cot_ref, cot_sem)
    cot_load.start()
    for d in range(tiles):
        for c in loads(d):
            c.start()
    cot_load.wait()

    def step(d, carry):
        for c in loads(d):
            c.wait()
        keep(d).start()
        terms = jnp.dot(cot_ref[...], rows_ref[:, columns(d)], preferred_element_type=jnp.float32) * scale
        cut_ref[2 * d] = terms[:, :LANES].astype(jnp.bfloat16)
        cut_ref[2 * d + 1] = terms[:, LANES:].astype(jnp.bfloat16)
        return carry

    lax.fori_loop(0, tiles, step, 0)
    if apart:
        outs = [
            pltpu.make_async_copy(cut_ref.at[at_ref[owners_at + i]], out, out_sem.at[i]) for i, out in enumerate(out_hbm)
        ]
    else:
        outs = [pltpu.make_async_copy(cut_ref, out_hbm[0], out_sem.at[0])]
    for c in outs:
        c.start()
    for c in outs:
        c.wait()
    for d in range(tiles):
        keep(d).wait()


def features_body(rows0, rows1, one_hbm, two_hbm, feat_one, feat_two, rows_ref, one_ref, two_ref, out_one, out_two, sem, row_sem, out_sem):
    count = rows0.shape[0]
    step = 512
    loads = []
    for half in range(2):
        loads.append(pltpu.make_async_copy(one_hbm.at[:, half], one_ref.at[half], sem.at[half, 0]))
        loads.append(pltpu.make_async_copy(two_hbm.at[:, half], two_ref.at[half], sem.at[half, 1]))
    for c in loads:
        c.start()

    def row_loads(i):
        at = pl.ds(i * step if isinstance(i, int) else pl.multiple_of(i * step, step), step)
        return [
            pltpu.make_async_copy(rows.at[at], rows_ref.at[half, at], row_sem.at[half, i])
            for half, rows in enumerate((rows0, rows1))
        ]

    def stores(i):
        at = pl.ds(i * step if isinstance(i, int) else pl.multiple_of(i * step, step), step)
        return [
            pltpu.make_async_copy(out_one.at[at], feat_one.at[at], out_sem.at[0, i]),
            pltpu.make_async_copy(out_two.at[at], feat_two.at[at], out_sem.at[1, i]),
        ]

    for i in range(count // step):
        for c in row_loads(i):
            c.start()
    for c in loads:
        c.wait()

    def body(i, carry):
        for c in row_loads(i):
            c.wait()
        at = pl.ds(pl.multiple_of(i * step, step), step)
        for w_ref, out_ref in ((one_ref, out_one), (two_ref, out_two)):
            for lo in range(0, w_ref.shape[-1], 256):
                total = [
                    jnp.dot(
                        rows_ref[half, at, :],
                        w_ref[half, :, :, lo : lo + 256].reshape(-1, 256),
                        preferred_element_type=jnp.float32,
                    )
                    for half in range(2)
                ]
                out_ref[at, lo : lo + 256] = (total[0] + total[1]).astype(jnp.bfloat16)
        for c in stores(i):
            c.start()
        return carry

    lax.fori_loop(0, count // step, body, 0)
    for i in range(count // step):
        for c in stores(i):
            c.wait()


def total_of(pieces):
    total = pieces[0].astype(jnp.float32)
    for piece in pieces[1:]:
        total = total + piece.astype(jnp.float32)
    return total.T


def sums_body(first_ref, *refs):
    *pieces, one_ref, two_ref = refs
    split = one_ref.shape[1]
    halves = [[first_ref[i] for i in range(first_ref.shape[0])], [piece[...] for piece in pieces]]
    for k, half in enumerate(halves):
        total = total_of(half)
        one_ref[k * LANES : (k + 1) * LANES] = total[:, :split]
        two_ref[k * LANES : (k + 1) * LANES] = total[:, split:]


STEPS = [(0, 0), (2, 1), (2, 0), (1, 1), (3, 1), (1, 0), (3, 0), (0, 1)]
RING = 4


def gathered_spots(place, rows):
    z, y_lo, y_hi, x, core = place

    def row_of(y, at, c):
        return (y * RING + at % RING) * (2 * rows) + c * rows

    def single(y, first):
        half = rows // 2
        out = []
        for k, c in enumerate((core, 1 - core)):
            at = first + 5 * k
            out += [(at + i, 0, rows, row_of(y, x + d, c)) for i, d in enumerate((0, RING - 1, 1))]
            out += [(at + 3 + i, 0, half, row_of(y, x + 2, c) + i * half) for i in range(2)]
        return out

    def double(first):
        out = []
        for k, c in enumerate((core, 1 - core)):
            at = first + 5 * k
            for side, y in enumerate((y_hi, 1 - y_hi)):
                out += [(at + i, side * rows, rows, row_of(y, x + d, c)) for i, d in enumerate((0, RING - 1, 1))]
                out.append((at + 3 + side, 0, rows, row_of(y, x + 2, c)))
        return out

    owners = [(z + dz) % 4 * 2 + (y_lo + dy) % 2 for dz, dy in STEPS]
    return single(y_hi, 0) + single(1 - y_hi, 10), double(0), owners


def spots_table(place, rows):
    first, second, owners = gathered_spots(place, rows)
    return jnp.stack([spot[3] for spot in first + second] + owners).astype(jnp.int32)


def project(parts, student_one, student_two, cots, move, pass_on, place, table):
    rows, half_width = parts[0].shape
    spots0, spots1, _ = gathered_spots(place, rows)
    owners = len(STEPS)
    count = 4 * RING * rows
    split = student_one.shape[1]
    cols = split + student_two.shape[1]
    bf16, f32 = jnp.bfloat16, jnp.float32
    dma = pltpu.SemaphoreType.DMA
    anywhere = pl.BlockSpec(memory_space=pl.ANY)
    inside = pl.BlockSpec(memory_space=pltpu.VMEM)

    def gather(block):
        half = block.shape[0] // 2
        right = move(block, 0, 1, 0)
        left = move(block, 0, -1, 0)
        far_right = move(right[:half], 0, 1, 0)
        far_left = move(left[half:], 0, -1, 0)
        own = [block, right, left, far_right, far_left]
        swapped = []
        for piece in own:
            swapped.append(move(piece, 0, 0, 1))
        return own + swapped

    def terms(pieces, spots, base, apart):
        cuts = (owners * [jax.ShapeDtypeStruct((cols, LANES), bf16)]) if apart else [
            jax.ShapeDtypeStruct((owners, cols, LANES), bf16)
        ]
        blocks = tuple(spot[:3] for spot in spots)
        return pl.pallas_call(
            functools.partial(
                terms_body,
                pieces=len(pieces),
                blocks=blocks,
                base=base,
                owners_at=table.shape[0] - owners,
                scale=1.0 / math.sqrt(count * owners),
                apart=apart,
            ),
            name="terms",
            grid_spec=pltpu.PrefetchScalarGridSpec(
                num_scalar_prefetch=1,
                grid=(1,),
                in_specs=[anywhere] * (len(pieces) + 1),
                out_specs=(anywhere,) * (len(cuts) + 1),
                scratch_shapes=[
                    pltpu.VMEM((count, half_width), bf16),
                    pltpu.VMEM((cols, count), bf16),
                    pltpu.VMEM((owners, cols, LANES), bf16),
                    dma((owners // 2, len(blocks))),
                    dma((owners // 2,)),
                    dma,
                    dma((owners,)),
                ],
            ),
            out_shape=(*cuts, jax.ShapeDtypeStruct((count, half_width), bf16)),
            compiler_params=pltpu.CompilerParams(vmem_limit_bytes=VMEM_LIMIT),
            cost_estimate=pl.CostEstimate(
                flops=2 * count * half_width * cols, transcendentals=0, bytes_accessed=12 << 20
            ),
        )(table, *pieces, cots)

    other0 = move(parts[0], 2, 0, 0)
    other1 = move(parts[1], 2, 0, 0)
    cut0, rows0 = terms(gather(parts[0]) + gather(other0), spots0, 0, False)
    cut0 = lax.all_to_all(cut0, "dp", split_axis=0, concat_axis=0, tiled=True)
    *cut1, rows1 = terms(gather(jnp.concatenate([parts[1], other1], axis=0)), spots1, len(spots0), True)
    for i, (dz, dy) in enumerate(STEPS[1:], 1):
        cut1[i] = pass_on(cut1[i], dz, dy)
    shape = (owners, 2, LANES)
    feat_one, feat_two = pl.pallas_call(
        features_body,
        name="features",
        in_specs=[anywhere] * 4,
        out_specs=(anywhere, anywhere),
        out_shape=(
            jax.ShapeDtypeStruct((count, split), bf16),
            jax.ShapeDtypeStruct((count, cols - split), bf16),
        ),
        scratch_shapes=[
            pltpu.VMEM((2, count, half_width), bf16),
            pltpu.VMEM((2, owners, LANES, split), bf16),
            pltpu.VMEM((2, owners, LANES, cols - split), bf16),
            pltpu.VMEM((count, split), bf16),
            pltpu.VMEM((count, cols - split), bf16),
            dma((2, 2)),
            dma((2, count // 512)),
            dma((2, count // 512)),
        ],
        compiler_params=pltpu.CompilerParams(vmem_limit_bytes=VMEM_LIMIT),
        cost_estimate=pl.CostEstimate(flops=4 * count * half_width * cols, transcendentals=0, bytes_accessed=14 << 20),
    )(rows0, rows1, student_one.reshape(*shape, split), student_two.reshape(*shape, cols - split))
    grad_one, grad_two = pl.pallas_call(
        sums_body,
        name="sums",
        in_specs=[inside] * (1 + owners),
        out_specs=(inside, inside),
        out_shape=(
            jax.ShapeDtypeStruct((2 * LANES, split), f32),
            jax.ShapeDtypeStruct((2 * LANES, cols - split), f32),
        ),
    )(cut0, *cut1)
    return feat_one, feat_two, grad_one, grad_two


def local(
    tokens,
    norm_gain,
    expert_ids,
    gate_weights,
    gate_proj,
    up_proj,
    down_proj,
    student_one,
    student_two,
    cot_one,
    cot_two,
):
    tok_dev, model_width = tokens.shape
    top_count = expert_ids.shape[1]
    devices = lax.axis_size("dp") * lax.axis_size("expert")
    experts = devices // 2
    capacity = 2 * ((tok_dev * top_count * 7 + 12 * experts - 1) // (12 * experts))
    sub = model_width // LANES
    axes = ("dp", "expert")
    index = lax.axis_index(axes)

    def move(array, y, x, core):
        def target(d):
            z, y_lo, y_hi, at_x, at_core = d // 32, d // 16 % 2, d // 8 % 2, d // 2 % 4, d % 2
            to_y = (y_hi * 2 + y_lo + y) % 4
            return z * 32 + to_y % 2 * 16 + to_y // 2 * 8 + (at_x + x) % 4 * 2 + (at_core + core) % 2

        return lax.ppermute(array, axes, [(d, target(d)) for d in range(devices)])

    def pass_on(array, z, y_lo):
        def target(d):
            return (d // 32 + z) % 4 * 32 + (d // 16 + y_lo) % 2 * 16 + d % 16

        return lax.ppermute(array, axes, [(d, target(d)) for d in range(devices)])

    cots = jnp.concatenate([cot_one, cot_two], axis=1).T
    other_gate = move(jnp.swapaxes(gate_proj[0], 0, 1), 0, 0, 1)
    other_up = move(jnp.swapaxes(up_proj[0], 0, 1), 0, 0, 1)
    place = (index // 32, index // 16 % 2, index // 8 % 2, index // 2 % 4, index % 2)
    table = spots_table(place, tok_dev)
    other_down, cots, table = lax.optimization_barrier((move(down_proj[0], 0, 0, 1), cots, table))

    placed, positions = dispatch(expert_ids.T, tokens, norm_gain.reshape(1, -1), experts, capacity)
    received = lax.all_to_all(
        placed.reshape(devices, capacity // 2, sub, LANES),
        ("dp", "expert"),
        split_axis=0,
        concat_axis=0,
        tiled=True,
    )
    expert_out = expert(
        received.reshape(devices * capacity // 2, sub, LANES),
        jnp.swapaxes(gate_proj[0], 0, 1),
        jnp.swapaxes(up_proj[0], 0, 1),
        down_proj[0],
        other_gate,
        other_up,
        other_down,
    )
    returned = lax.all_to_all(
        expert_out.reshape(devices, capacity // 2, sub, LANES),
        ("dp", "expert"),
        split_axis=0,
        concat_axis=0,
        tiled=True,
    )
    layer_out, *parts = combine(positions, gate_weights.T, returned.reshape(experts * capacity, sub, LANES))
    feat_one, feat_two, grad_one, grad_two = project(parts, student_one, student_two, cots, move, pass_on, place, table)
    return (layer_out, feat_one, feat_two, grad_one, grad_two)


def solution(mesh):
    return jax.shard_map(
        local,
        mesh=mesh,
        in_specs=(
            P(("dp", "expert"), None),
            P(),
            P(("dp", "expert"), None),
            P(("dp", "expert"), None),
            P(("dp", "expert"), None, None),
            P(("dp", "expert"), None, None),
            P(("dp", "expert"), None, None),
            P(None, "expert"),
            P(None, "expert"),
            P("dp", "expert"),
            P("dp", "expert"),
        ),
        out_specs=(
            P(("dp", "expert"), None),
            P("dp", "expert"),
            P("dp", "expert"),
            P("dp", "expert"),
            P("dp", "expert"),
        ),
        check_vma=False,
    )
```
